128 devices in a mesh: row: 8 (over x, z_lo), col: 16 (over z_hi, y, core).
Axes of the slice: x: 4, y: 4, z: 4 (z_hi: 2, z_lo: 2; z = z_hi * 2 + z_lo), core: 2. Of those that a mesh axis runs over, the one named last changes fastest.
Arguments:
- pair: bfloat16 [512, 512, 128], P('row', 'col'), may hold values from -6 to 6
- cotangent: bfloat16 [512, 512, 128], P('row', 'col'), may hold values from -6 to 6
- res_mask: int32 [512], replicated, may hold values 0 or 1
- chain: int32 [512], replicated, may hold values from 0 to 3, never falling along the last dimension, each value on 1 to 256 neighbouring positions
- ln_in_gain: float32 [128], replicated, may hold values from 0.5 to 1.5
- ln_in_bias: float32 [128], replicated, may hold values from -3 to 3
- w_proj: bfloat16 [128, 512], replicated, may hold values from -0.5 to 0.5
- w_gate: bfloat16 [128, 128], replicated, may hold values from -0.5 to 0.5
- chain_bias: float32 [128], replicated, may hold values from -4 to 4
- ln_out_gain: float32 [128], replicated, may hold values from 0.5 to 1.5
- ln_out_bias: float32 [128], replicated, may hold values from -3 to 3
- w_out: bfloat16 [128, 128], replicated, may hold values from -0.5 to 0.5
Outputs:
- grad_pair: bfloat16 [512, 512, 128], P('row', 'col')
- grad_proj: float32 [128, 512], replicated
- grad_gate: float32 [128, 128], replicated
- grad_out: float32 [128, 128], replicated
The draws below stay inside these ranges and needn't reach their ends.
Inputs may be any that keep to these rules, and one draw needn't show every extreme that they name: chain never decreases along the residues.
All inputs are finite; a program needn't handle non-finite values.
Results may differ from the reference program's by a relative error of at most 0.02.
Values may be sent and summed in bfloat16 or wider, within the bound.
No kernel may reach another device: no remote copies, remote signals or barrier semaphores. Data moves between devices by JAX's collectives and lax.ppermute only.
A program may use at most 128 MiB of HBM per device.

```python
import math
import jax
import jax.numpy as jnp
import numpy as np
from jax import lax

C = 128
H = 128
ROWS_DEV = 64
N = 512


def place_ends(drawn, stream_key, least, largest):
    spot = [jax.random.randint(jax.random.fold_in(stream_key, axis), (), 0, length) for axis, length in enumerate(drawn.shape)]
    widest = drawn.shape.index(max(drawn.shape))
    beside = spot[:widest] + [(spot[widest] + 1) % drawn.shape[widest]] + spot[widest + 1:]
    return drawn.at[tuple(spot)].set(least).at[tuple(beside)].set(largest)


def levels(key, extent, cuts, low, top_value):
    factor_of, own = 1.0, jax.random.fold_in(key, 6)
    for position, shards_of in cuts:
        heights = jnp.exp(jax.random.uniform(jax.random.fold_in(own, position), (shards_of,), jnp.float32, low / len(cuts), top_value / len(cuts)))
        factor_of = factor_of * jnp.repeat(heights, extent[position] // shards_of).reshape([-1 if axis == position else 1 for axis in range(len(extent))])
    return factor_of


def profile(count, total, most, skew):
    loads = [(1 << 20) // math.isqrt(rank ** skew) + 1 for rank in range(2, count + 1)]
    rest, holding = total - most - (count - 1), [1] * (count - 1)
    while rest > 0:
        candidates = [i for i in range(count - 1) if holding[i] < most]
        whole, left = sum([loads[i] for i in candidates]), rest
        for i in candidates:
            addition = min(most - holding[i], max(1, left * loads[i] // whole), rest)
            holding[i] = holding[i] + addition
            rest = rest - addition
    return np.array([most] + holding)


def ragged_sizes(own_key, number_of, total, most, slope):
    if number_of == 2:
        one = jax.random.randint(own_key, (), max(1, total - most), min(most, total - 1) + 1)
        return jnp.stack([one, total - one])
    sizes = jnp.asarray(profile(number_of, total, most, slope), jnp.int32)
    couples = (number_of - 1) // 2
    donor, sink = sizes[1:1 + 2 * couples:2], sizes[2:2 + 2 * couples:2]
    room = jnp.minimum(donor - 1, most - sink)
    passed = jax.random.randint(jax.random.fold_in(own_key, 1), (couples,), 0, 1 << 20) % (room + 1)
    sizes = sizes.at[1:1 + 2 * couples:2].set(donor - passed).at[2:2 + 2 * couples:2].set(sink + passed)
    return sizes[jax.random.permutation(jax.random.fold_in(own_key, 2), number_of)]


def gaussian(own_key, dims, deviation, reach, cuts=(), held_as=jnp.bfloat16):
    entries = deviation * jax.random.normal(own_key, dims, jnp.float32)
    if cuts:
        entries = entries * levels(own_key, dims, cuts, -0.22, 0.18)
    return jnp.clip(entries, -reach, reach).astype(held_as)


def setup_inputs(seed: int = 0) -> dict:
    key_of = jax.random.split(jax.random.key(seed), 13)
    return {
        "pair": gaussian(key_of[0], (N, N, C), 1.0, 6.0, ((0, 8), (1, 16))),
        "cotangent": gaussian(key_of[1], (N, N, C), 1.0, 6.0, ((0, 8), (1, 16))),
        "res_mask": place_ends((jax.random.randint(key_of[2], (N,), 0, 8) < 7).astype(jnp.int32), jax.random.fold_in(key_of[2], 1), 0, 1),
        "chain": jnp.searchsorted(jnp.cumsum(ragged_sizes(key_of[3], 4, N, N // 2, 1)), jnp.arange(N), side="right").astype(jnp.int32),
        "ln_in_gain": jnp.clip(1.0 + 0.1 * jax.random.normal(key_of[4], (C,), jnp.float32), 0.5, 1.5),
        "ln_in_bias": gaussian(key_of[5], (C,), 0.5, 3.0, (), jnp.float32),
        "w_proj": gaussian(key_of[6], (C, 4 * H), C ** -0.5, 0.5),
        "w_gate": gaussian(key_of[7], (C, C), C ** -0.5, 0.5),
        "chain_bias": gaussian(key_of[8], (C,), 1.0, 4.0, (), jnp.float32),
        "ln_out_gain": jnp.clip(1.0 + 0.1 * jax.random.normal(key_of[9], (H,), jnp.float32), 0.5, 1.5),
        "ln_out_bias": gaussian(key_of[10], (H,), 0.5, 3.0, (), jnp.float32),
        "w_out": gaussian(key_of[11], (H, C), H ** -0.5, 0.5),
    }


EPS = 1e-05

def layer_norm(values, gain, bias):
    mean = lax.optimization_barrier(jnp.mean(values, axis=-1, keepdims=True))
    centred = values - mean
    inverse = lax.rsqrt(lax.optimization_barrier(jnp.mean(centred * centred, axis=-1, keepdims=True)) + EPS)
    normed = centred * inverse
    return (normed * gain + bias, normed, inverse)

def norm_back(grad_normed, normed, inverse):
    first = lax.optimization_barrier(jnp.mean(grad_normed, axis=-1, keepdims=True))
    second = lax.optimization_barrier(jnp.mean(grad_normed * normed, axis=-1, keepdims=True))
    return (grad_normed - first - normed * second) * inverse

def matmul_last(left, right):
    shape = left.shape
    flat = jnp.dot(left.reshape(-1, shape[-1]), right, preferred_element_type=jnp.float32)
    return flat.reshape(shape[:-1] + (right.shape[1],))

def contract_pairs(left, right):
    flat_left = left.reshape(-1, left.shape[-1])
    flat_right = right.reshape(-1, right.shape[-1])
    return lax.dot_general(flat_left, flat_right, (((0,), (0,)), ((), ())), preferred_element_type=jnp.float32)

def project(pair, ln_in_gain, ln_in_bias, w_proj):
    scaled, normed, inverse = layer_norm(pair.astype(jnp.float32), ln_in_gain, ln_in_bias)
    normed_b = scaled.astype(jnp.bfloat16)
    return (normed_b, normed, inverse, matmul_last(normed_b, w_proj))

def activations(proj, pair_mask):
    width = proj.shape[-1] // 4
    gate_a = jax.nn.sigmoid(proj[..., :width])
    gate_b = jax.nn.sigmoid(proj[..., 2 * width:3 * width])
    act_a = (gate_a * proj[..., width:2 * width] * pair_mask).astype(jnp.bfloat16)
    act_b = (gate_b * proj[..., 3 * width:] * pair_mask).astype(jnp.bfloat16)
    return (act_a, act_b)

def gated_output(mixed, cotangent, normed_b, same, chain_bias, w_gate, ln_out_gain, ln_out_bias, w_out):
    scaled, normed, inverse = layer_norm(mixed, ln_out_gain, ln_out_bias)
    out_b = scaled.astype(jnp.bfloat16)
    update = matmul_last(out_b, w_out)
    gate = jax.nn.sigmoid(matmul_last(normed_b, w_gate) + same * chain_bias)
    cot = cotangent.astype(jnp.float32)
    grad_update = (cot * gate).astype(jnp.bfloat16)
    grad_logit = (cot * update * gate * (1.0 - gate)).astype(jnp.bfloat16)
    grad_scaled = matmul_last(grad_update, w_out.T)
    grad_mixed = norm_back(grad_scaled * ln_out_gain, normed, inverse).astype(jnp.bfloat16)
    return (grad_mixed, grad_logit, contract_pairs(out_b, grad_update), contract_pairs(normed_b, grad_logit))

def input_back(normed_b, normed, inverse, proj, pair_mask, grad_a, grad_b, grad_logit, ln_in_gain, w_proj, w_gate):
    width = proj.shape[-1] // 4
    gate_a = jax.nn.sigmoid(proj[..., :width])
    gate_b = jax.nn.sigmoid(proj[..., 2 * width:3 * width])
    masked_a = grad_a * pair_mask
    masked_b = grad_b * pair_mask
    grad_p = jnp.concatenate([masked_a * proj[..., width:2 * width] * gate_a * (1.0 - gate_a), masked_a * gate_a, masked_b * proj[..., 3 * width:] * gate_b * (1.0 - gate_b), masked_b * gate_b], axis=-1).astype(jnp.bfloat16)
    grad_zn = matmul_last(grad_p, w_proj.T) + matmul_last(grad_logit, w_gate.T)
    grad_pair = norm_back(grad_zn * ln_in_gain, normed, inverse).astype(jnp.bfloat16)
    return (grad_pair, contract_pairs(normed_b, grad_p))

def reference(pair, cotangent, res_mask, chain, ln_in_gain, ln_in_bias, w_proj, w_gate, chain_bias, ln_out_gain, ln_out_bias, w_out):
    blocks = N // ROWS_DEV
    maskf = res_mask.astype(jnp.float32)

    def split(values):
        return values.reshape((blocks, ROWS_DEV) + values.shape[1:])

    def first(items):
        pair_rows, mask_rows = items
        pair_mask = mask_rows[:, None, None] * maskf[None, :, None]
        proj = project(pair_rows, ln_in_gain, ln_in_bias, w_proj)[3]
        return activations(proj, pair_mask)
    act_a, act_b = lax.map(first, (split(pair), split(maskf)))
    act_a = act_a.reshape(N, N, H)
    act_b = act_b.reshape(N, N, H)
    mixed = jnp.einsum('ikh,jkh->ijh', act_a.astype(jnp.float32), act_b.astype(jnp.float32))

    def second(items):
        mixed_rows, cot_rows, pair_rows, chain_rows = items
        normed_b = project(pair_rows, ln_in_gain, ln_in_bias, w_proj)[0]
        same = (chain_rows[:, None] == chain[None, :]).astype(jnp.float32)[:, :, None]
        return gated_output(mixed_rows, cot_rows, normed_b, same, chain_bias, w_gate, ln_out_gain, ln_out_bias, w_out)
    grad_mixed, grad_logit, terms_out, terms_gate = lax.map(second, (split(mixed), split(cotangent), split(pair), split(chain)))
    grad_mixed = grad_mixed.reshape(N, N, H)
    grad_a = jnp.einsum('ijh,jkh->ikh', grad_mixed.astype(jnp.float32), act_b.astype(jnp.float32))
    grad_b = jnp.einsum('ijh,ikh->jkh', grad_mixed.astype(jnp.float32), act_a.astype(jnp.float32))

    def third(items):
        pair_rows, mask_rows, grad_a_rows, grad_b_rows, logit_rows = items
        pair_mask = mask_rows[:, None, None] * maskf[None, :, None]
        normed_b, normed, inverse, proj = project(pair_rows, ln_in_gain, ln_in_bias, w_proj)
        return input_back(normed_b, normed, inverse, proj, pair_mask, grad_a_rows, grad_b_rows, logit_rows, ln_in_gain, w_proj, w_gate)
    grad_pair, terms_proj = lax.map(third, (split(pair), split(maskf), split(grad_a), split(grad_b), grad_logit))
    scale = 1.0 / N
    return (grad_pair.reshape(N, N, C), lax.optimization_barrier(jnp.sum(terms_proj, axis=0)) * scale, lax.optimization_barrier(jnp.sum(terms_gate, axis=0)) * scale, lax.optimization_barrier(jnp.sum(terms_out, axis=0)) * scale)
```

```python
import functools

import jax
import jax.numpy as jnp
from jax import lax
from jax.experimental import pallas as pl
from jax.experimental.pallas import tpu as pltpu
from jax.sharding import PartitionSpec as P

EPS = 1e-05
F32 = jnp.float32
BF16 = jnp.bfloat16
AXES = ("row", "col")

ROWS = 64
COLS = 32
NROW = 8
NCOL = 16
DEV = NROW * NCOL
CH = 128
N = 512
PAIRS = ROWS * COLS
LANES = 128
CHUNKS = PAIRS // LANES
TILES = N // LANES


def dot(left, right, dim_left, dim_right):
    return lax.dot_general(
        left, right, (((dim_left,), (dim_right,)), ((), ())), preferred_element_type=F32
    )


def sigmoid(x):
    return 0.5 * jnp.tanh(0.5 * x) + 0.5


def column(row):
    return jnp.broadcast_to(row, (LANES, row.shape[1])).T


def lanes_of(s, offset=0):
    return pl.ds(pl.multiple_of(s * LANES + offset, LANES), LANES)


def swap_halves(first, second):
    low = lax.broadcasted_iota(jnp.int32, first.shape, 1) < LANES // 2
    return (
        jnp.where(low, first, pltpu.roll(second, LANES // 2, 1)),
        jnp.where(low, pltpu.roll(first, LANES // 2, 1), second),
    )


def load_chunk(ref, s):
    top = ref[pl.ds(2 * s, ROWS, stride=COLS), :]
    bottom = ref[pl.ds(2 * s + 1, ROWS, stride=COLS), :]
    return jnp.concatenate([top, bottom], axis=0)


def front_kernel(mask_s, chain_s, pair, gain, bias, w_proj, send, zn_t, normed_t, aux, xs, w_t):
    row_start = lax.axis_index("row") * ROWS
    col_start = lax.axis_index("col") * COLS
    xs[...] = pair[...].astype(F32).reshape(PAIRS, CH)
    w_t[...] = w_proj[...].astype(F32).T.astype(BF16)
    gain_c = column(gain[...])
    bias_c = column(bias[...])
    lane = lax.broadcasted_iota(jnp.int32, (1, LANES), 1)
    place = lane % ROWS
    mask_row = jnp.zeros((1, LANES), jnp.int32)
    chain_row = jnp.zeros((1, LANES), jnp.int32)
    for i in range(ROWS):
        here = place == i
        mask_row = jnp.where(here, mask_s[row_start + i], mask_row)
        chain_row = jnp.where(here, chain_s[row_start + i], chain_row)
    low = lane < ROWS

    def step(s, carry):
        x = load_chunk(xs, s).T
        mean = jnp.mean(x, axis=0, keepdims=True)
        centred = x - mean
        inverse = lax.rsqrt(jnp.mean(centred * centred, axis=0, keepdims=True) + EPS)
        normed = centred * inverse
        zn = (normed * gain_c + bias_c).astype(BF16)
        k = col_start + 2 * s
        mask = (jnp.where(low, mask_s[k], mask_s[k + 1]) * mask_row).astype(F32)
        same = (jnp.where(low, chain_s[k], chain_s[k + 1]) == chain_row).astype(F32)
        proj = dot(w_t[...], zn, 1, 0)
        act_a = sigmoid(proj[:CH]) * proj[CH : 2 * CH] * mask
        act_b = sigmoid(proj[2 * CH : 3 * CH]) * proj[3 * CH :] * mask
        send[:, lanes_of(s)] = act_a.astype(BF16)
        send[:, lanes_of(s, PAIRS)] = act_b.astype(BF16)
        zn_t[:, lanes_of(s)] = zn
        normed_t[:, lanes_of(s)] = normed
        aux[0:1, lanes_of(s)] = mask
        aux[1:2, lanes_of(s)] = same
        aux[2:3, lanes_of(s)] = inverse
        return carry

    lax.fori_loop(0, CHUNKS, step, 0)


def mix_kernel(recv, send, a_t, b_t, mixed):
    def gather(s, carry):
        for t in range(TILES):
            for offset, out in ((0, a_t), (PAIRS, b_t)):
                first = recv[32 * t : 32 * t + 16, lanes_of(s, offset)].astype(F32)
                second = recv[32 * t + 16 : 32 * t + 32, lanes_of(s, offset)].astype(F32)
                even, odd = swap_halves(first, second)
                spot = slice(t * LANES, (t + 1) * LANES)
                row = pl.multiple_of(s * 32, 32)
                out[pl.ds(row, 16), spot] = even.astype(BF16)
                out[pl.ds(row + 16, 16), spot] = odd.astype(BF16)
        return carry

    lax.fori_loop(0, CHUNKS, gather, 0)
    for t in range(TILES):
        spot = slice(t * LANES, (t + 1) * LANES)
        mixed[t] = dot(b_t[...], a_t[:, spot], 0, 0)

    def scatter(s, carry):
        for t in range(TILES):
            first = mixed[t, pl.ds(2 * s, NCOL, stride=COLS), :]
            second = mixed[t, pl.ds(2 * s + 1, NCOL, stride=COLS), :]
            even, odd = swap_halves(first, second)
            send[32 * t : 32 * t + 16, lanes_of(s)] = even.astype(BF16)
            send[32 * t + 16 : 32 * t + 32, lanes_of(s)] = odd.astype(BF16)
        return carry

    lax.fori_loop(0, CHUNKS, scatter, 0)


def middle_kernel(
    recv, cot, zn_t, aux, w_gate, chain_bias, gain, bias, w_out,
    send, logit_t, cs, wg_t, wo_t, term_out, term_gate,
):
    cs[...] = cot[...].astype(F32).reshape(PAIRS, CH)
    wg_t[...] = w_gate[...].astype(F32).T.astype(BF16)
    wo_t[...] = w_out[...].astype(F32).T.astype(BF16)
    gain_c = column(gain[...])
    bias_c = column(bias[...])
    chain_c = column(chain_bias[...])
    term_out[...] = jnp.zeros_like(term_out)
    term_gate[...] = jnp.zeros_like(term_gate)

    def step(s, carry):
        here = lanes_of(s)
        mixed = recv[:, here].astype(F32)
        mean = jnp.mean(mixed, axis=0, keepdims=True)
        centred = mixed - mean
        inverse = lax.rsqrt(jnp.mean(centred * centred, axis=0, keepdims=True) + EPS)
        normed = centred * inverse
        y = (normed * gain_c + bias_c).astype(BF16)
        zn = zn_t[:, here]
        update = dot(wo_t[...], y, 1, 0)
        gate = sigmoid(dot(wg_t[...], zn, 1, 0) + aux[1:2, here] * chain_c)
        cot_t = load_chunk(cs, s).T
        grad_gated = cot_t * gate
        grad_update = grad_gated.astype(BF16)
        grad_logit = (grad_gated * update * (1.0 - gate)).astype(BF16)
        q = dot(w_out[...], grad_update, 1, 0) * gain_c
        first = jnp.mean(q, axis=0, keepdims=True)
        second = jnp.mean(q * normed, axis=0, keepdims=True)
        grad_mixed = (q - first - normed * second) * inverse
        send[:, here] = grad_mixed.astype(BF16)
        logit_t[:, here] = grad_logit
        term_out[...] += dot(y, grad_update, 1, 1)
        term_gate[...] += dot(zn, grad_logit, 1, 1)
        return carry

    lax.fori_loop(0, CHUNKS, step, 0)
    send[:, PAIRS : PAIRS + CH] = term_out[...].astype(BF16)
    send[:, PAIRS + CH : PAIRS + 2 * CH] = term_gate[...].astype(BF16)


def unmix_kernel(recv, a_t, b_t, send, strided, grad, product):
    def gather(s, carry):
        for t in range(TILES):
            first = recv[32 * t : 32 * t + 16, lanes_of(s)].astype(F32)
            second = recv[32 * t + 16 : 32 * t + 32, lanes_of(s)].astype(F32)
            even, odd = swap_halves(first, second)
            strided[t, pl.ds(2 * s, NCOL, stride=COLS), :] = even
            strided[t, pl.ds(2 * s + 1, NCOL, stride=COLS), :] = odd
        return carry

    lax.fori_loop(0, CHUNKS, gather, 0)
    for t in range(TILES):
        grad[:, t * LANES : (t + 1) * LANES] = strided[t].astype(BF16)
    for offset, left, dim in ((0, b_t, 0), (PAIRS, a_t, 1)):
        product[...] = dot(left[...], grad[...], 1, dim)

        def scatter(s, carry):
            row = pl.multiple_of(s * 32, 32)
            for t in range(TILES):
                spot = slice(t * LANES, (t + 1) * LANES)
                even, odd = swap_halves(
                    product[pl.ds(row, 16), spot], product[pl.ds(row + 16, 16), spot]
                )
                send[32 * t : 32 * t + 16, lanes_of(s, offset)] = even.astype(BF16)
                send[32 * t + 16 : 32 * t + 32, lanes_of(s, offset)] = odd.astype(BF16)
            return carry

        lax.fori_loop(0, CHUNKS, scatter, 0)
    terms = recv[:, PAIRS : PAIRS + 2 * CH].astype(F32)
    total = jnp.sum(terms, axis=0, keepdims=True) * (1.0 / N)
    high = total.astype(BF16)
    rest = (total - high.astype(F32)).astype(BF16)
    wide = (DEV, 2 * CH)
    send[:, 2 * PAIRS : 2 * PAIRS + 2 * CH] = jnp.broadcast_to(high.astype(F32), wide).astype(BF16)
    send[:, 2 * PAIRS + 2 * CH :] = jnp.broadcast_to(rest.astype(F32), wide).astype(BF16)


def back_kernel(
    recv, zn_t, normed_t, aux, logit_t, gain, w_proj, w_gate,
    grad_pair, term_proj, grad_gate, grad_out, ys, w_t,
):
    w_t[...] = w_proj[...].astype(F32).T.astype(BF16)
    gain_c = column(gain[...])
    term_proj[...] = jnp.zeros_like(term_proj)

    def step(s, carry):
        here = lanes_of(s)
        zn = zn_t[:, here]
        mask = aux[0:1, here]
        inverse = aux[2:3, here]
        proj = dot(w_t[...], zn, 1, 0)
        gate_a = sigmoid(proj[:CH])
        gate_b = sigmoid(proj[2 * CH : 3 * CH])
        gated_a = recv[:, here].astype(F32) * mask * gate_a
        gated_b = recv[:, lanes_of(s, PAIRS)].astype(F32) * mask * gate_b
        grad_p = jnp.concatenate(
            [
                gated_a * proj[CH : 2 * CH] * (1.0 - gate_a),
                gated_a,
                gated_b * proj[3 * CH :] * (1.0 - gate_b),
                gated_b,
            ],
            axis=0,
        ).astype(BF16)
        term_proj[...] += dot(zn, grad_p, 1, 1)
        grad_zn = dot(w_proj[...], grad_p, 1, 0) + dot(w_gate[...], logit_t[:, here], 1, 0)
        normed = normed_t[:, here]
        q = grad_zn * gain_c
        first = jnp.mean(q, axis=0, keepdims=True)
        second = jnp.mean(q * normed, axis=0, keepdims=True)
        out = ((q - first - normed * second) * inverse).T
        ys[pl.ds(2 * s, ROWS, stride=COLS), :] = out[:ROWS]
        ys[pl.ds(2 * s + 1, ROWS, stride=COLS), :] = out[ROWS:]
        return carry

    lax.fori_loop(0, CHUNKS, step, 0)
    grad_pair[...] = ys[...].reshape(ROWS, COLS, CH).astype(BF16)
    base = 2 * PAIRS
    total = recv[:, base : base + 2 * CH].astype(F32) + recv[:, base + 2 * CH :].astype(F32)
    grad_out[...] = total[:, :CH]
    grad_gate[...] = total[:, CH:]


def sum_kernel(parts, out):
    total = jnp.sum(parts[...], axis=0, keepdims=True) * (1.0 / N)
    out[...] = jnp.broadcast_to(total, out.shape)


def call(kernel, outs, scratch, flops, args, smem=0):
    specs = [pl.BlockSpec(memory_space=pltpu.SMEM)] * smem
    specs += [pl.BlockSpec(memory_space=pltpu.VMEM)] * (len(args) - smem)
    moved = sum(x.size * x.dtype.itemsize for x in args) + sum(
        x.size * x.dtype.itemsize for x in outs
    )
    return pl.pallas_call(
        kernel,
        out_shape=outs,
        in_specs=specs,
        out_specs=[pl.BlockSpec(memory_space=pltpu.VMEM)] * len(outs),
        scratch_shapes=scratch,
        compiler_params=pltpu.CompilerParams(vmem_limit_bytes=48 << 20),
        cost_estimate=pl.CostEstimate(flops=flops, bytes_accessed=moved, transcendentals=0),
    )(*args)


def exchange(x):
    split = x.reshape(DEV, -1, LANES)
    return lax.all_to_all(split, AXES, 0, 0, tiled=True).reshape(x.shape)


def body(
    pair,
    cotangent,
    res_mask,
    chain,
    ln_in_gain,
    ln_in_bias,
    w_proj,
    w_gate,
    chain_bias,
    ln_out_gain,
    ln_out_bias,
    w_out,
):
    S = jax.ShapeDtypeStruct
    V = pltpu.VMEM

    def flat(x):
        return x.reshape(1, -1)

    send_ab, zn_t, normed_t, aux = call(
        front_kernel,
        [S((CH, 2 * PAIRS), BF16), S((CH, PAIRS), BF16), S((CH, PAIRS), F32), S((8, PAIRS), F32)],
        [V((PAIRS, CH), F32), V((4 * CH, CH), BF16)],
        2 * PAIRS * CH * 4 * CH,
        (res_mask, chain, pair, flat(ln_in_gain), flat(ln_in_bias), w_proj),
        smem=2,
    )
    send_mixed, a_t, b_t = call(
        mix_kernel,
        [S((DEV, PAIRS), BF16), S((N, N), BF16), S((N, N), BF16)],
        [V((TILES, N, LANES), F32)],
        2 * N * N * N,
        (exchange(send_ab),),
    )
    send_grad, logit_t = call(
        middle_kernel,
        [S((CH, PAIRS + 2 * CH), BF16), S((CH, PAIRS), BF16)],
        [V((PAIRS, CH), F32), V((CH, CH), BF16), V((CH, CH), BF16), V((CH, CH), F32), V((CH, CH), F32)],
        10 * PAIRS * CH * CH,
        (
            exchange(send_mixed), cotangent, zn_t, aux, w_gate, flat(chain_bias),
            flat(ln_out_gain), flat(ln_out_bias), w_out,
        ),
    )
    (send_back,) = call(
        unmix_kernel,
        [S((DEV, 2 * PAIRS + 4 * CH), BF16)],
        [V((TILES, N, LANES), F32), V((N, N), BF16), V((N, N), F32)],
        4 * N * N * N,
        (exchange(send_grad), a_t, b_t),
    )
    grad_pair, term_proj, grad_gate, grad_out = call(
        back_kernel,
        [S((ROWS, COLS, CH), BF16), S((CH, 4 * CH), F32), S((CH, CH), F32), S((CH, CH), F32)],
        [V((PAIRS, CH), F32), V((4 * CH, CH), BF16)],
        26 * PAIRS * CH * CH,
        (exchange(send_back), zn_t, normed_t, aux, logit_t, flat(ln_in_gain), w_proj, w_gate),
    )
    (summed,) = call(sum_kernel, [S((CH, 4 * CH), F32)], [], 0, (exchange(term_proj),))
    return (grad_pair, exchange(summed), grad_gate, grad_out)


def solution(mesh):
    return jax.shard_map(
        body,
        mesh=mesh,
        in_specs=(P("row", "col", None), P("row", "col", None)) + (P(),) * 10,
        out_specs=(P("row", "col", None), P(), P(), P()),
        check_vma=False,
    )
```

```python
import functools

import jax
import jax.numpy as jnp
from jax import lax
from jax.experimental import pallas as pl
from jax.experimental.pallas import tpu as pltpu
from jax.sharding import PartitionSpec as P

EPS = 1e-05
F32 = jnp.float32
BF16 = jnp.bfloat16
AXES = ("row", "col")

ROWS = 64
COLS = 32
NROW = 8
NCOL = 16
DEV = NROW * NCOL
CH = 128
N = 512
PAIRS = ROWS * COLS
LANES = 128
CHUNKS = PAIRS // LANES
WIDE = 256
STEPS = PAIRS // WIDE
EACH = WIDE // ROWS
TILES = N // LANES


def dot(left, right, dim_left, dim_right):
    return lax.dot_general(
        left, right, (((dim_left,), (dim_right,)), ((), ())), preferred_element_type=F32
    )


def sigmoid(x):
    return 0.5 * jnp.tanh(0.5 * x) + 0.5


def column(row):
    return jnp.broadcast_to(row, (WIDE, row.shape[1])).T


def lanes_of(s, offset=0):
    return pl.ds(pl.multiple_of(s * WIDE + offset, LANES), WIDE)


def swap_halves(first, second):
    low = lax.broadcasted_iota(jnp.int32, first.shape, 1) < LANES // 2
    return (
        jnp.where(low, first, pltpu.roll(second, LANES // 2, 1)),
        jnp.where(low, pltpu.roll(first, LANES // 2, 1), second),
    )


def load_chunk(ref, s):
    parts = [ref[pl.ds(EACH * s + e, ROWS, stride=COLS), :] for e in range(EACH)]
    return jnp.concatenate(parts, axis=0).T


def store_chunk(ref, s, value):
    value = value.T
    for e in range(EACH):
        ref[pl.ds(EACH * s + e, ROWS, stride=COLS), :] = value[e * ROWS : (e + 1) * ROWS]


def loop(step, unroll=2):
    def body(group, carry):
        for u in range(unroll):
            step(group * unroll + u)
        return carry

    lax.fori_loop(0, STEPS // unroll, body, 0)


def front_kernel(
    mask_h, chain_h, pair_h, gain_h, bias_h, w_h,
    send, zn_t, normed_t, aux,
    mask_s, chain_s, pair, gain, bias, w_proj, xs, w_t, sems,
):
    copies = [
        pltpu.make_async_copy(src, dst, sems.at[n])
        for n, (src, dst) in enumerate(
            (
                (pair_h, pair), (w_h, w_proj), (gain_h, gain), (bias_h, bias),
                (mask_h, mask_s), (chain_h, chain_s),
            )
        )
    ]
    for copy in copies:
        copy.start()
    for copy in copies[1:]:
        copy.wait()
    row_start = lax.axis_index("row") * ROWS
    col_start = lax.axis_index("col") * COLS
    w_t[...] = w_proj[...].astype(F32).T.astype(BF16)
    gain_c = column(gain[...])
    bias_c = column(bias[...])
    lane = lax.broadcasted_iota(jnp.int32, (1, LANES), 1)
    place = lane % ROWS
    mask_row = jnp.zeros((1, LANES), jnp.int32)
    chain_row = jnp.zeros((1, LANES), jnp.int32)
    for i in range(ROWS):
        here = place == i
        mask_row = jnp.where(here, mask_s[row_start + i], mask_row)
        chain_row = jnp.where(here, chain_s[row_start + i], chain_row)
    low = lane < ROWS
    copies[0].wait()
    xs[...] = pair[...].astype(F32).reshape(PAIRS, CH)

    def step(s):
        x = load_chunk(xs, s)
        mean = jnp.mean(x, axis=0, keepdims=True)
        centred = x - mean
        inverse = lax.rsqrt(jnp.mean(centred * centred, axis=0, keepdims=True) + EPS)
        normed = centred * inverse
        zn = (normed * gain_c + bias_c).astype(BF16)
        mask, same = [], []
        for e in range(0, EACH, 2):
            k = col_start + EACH * s + e
            mask.append((jnp.where(low, mask_s[k], mask_s[k + 1]) * mask_row).astype(F32))
            same.append((jnp.where(low, chain_s[k], chain_s[k + 1]) == chain_row).astype(F32))
        mask = jnp.concatenate(mask, axis=1)
        proj = dot(w_t[...], zn, 1, 0)
        act_a = sigmoid(proj[:CH]) * proj[CH : 2 * CH] * mask
        act_b = sigmoid(proj[2 * CH : 3 * CH]) * proj[3 * CH :] * mask
        send[:, lanes_of(s)] = act_a.astype(BF16)
        send[:, lanes_of(s, PAIRS)] = act_b.astype(BF16)
        zn_t[:, lanes_of(s)] = zn
        normed_t[:, lanes_of(s)] = normed
        aux[0:1, lanes_of(s)] = mask
        aux[1:2, lanes_of(s)] = jnp.concatenate(same, axis=1)
        aux[2:3, lanes_of(s)] = inverse

    loop(step)


def ahead_kernel(cot, zn_t, aux, w_gate, chain_bias, gain, w_out, grad_update, q_out, slope, cs, wg_t):
    cs[...] = cot[...].astype(F32).reshape(PAIRS, CH)
    wg_t[...] = w_gate[...].astype(F32).T.astype(BF16)
    gain_c = column(gain[...])
    chain_c = column(chain_bias[...])

    def step(s):
        here = lanes_of(s)
        gate = sigmoid(dot(wg_t[...], zn_t[:, here], 1, 0) + aux[1:2, here] * chain_c)
        gated = load_chunk(cs, s) * gate
        update = gated.astype(BF16)
        grad_update[:, here] = update
        slope[:, here] = gated * (1.0 - gate)
        q_out[:, here] = dot(w_out[...], update, 1, 0) * gain_c

    loop(step)


def mix_kernel(recv, send, a_t, b_t, mixed):
    for c in range(NCOL):
        for t in range(TILES):
            for offset, out in ((0, a_t), (CHUNKS, b_t)):
                rows = slice(offset, offset + CHUNKS)
                first = recv[32 * t + c, rows].astype(F32)
                second = recv[32 * t + 16 + c, rows].astype(F32)
                even, odd = swap_halves(first, second)
                spot = slice(t * LANES, (t + 1) * LANES)
                out[32 * c : 32 * c + 16, spot] = even.astype(BF16)
                out[32 * c + 16 : 32 * c + 32, spot] = odd.astype(BF16)
    product = dot(b_t[...], a_t[...], 0, 0)
    for t in range(TILES):
        mixed[t] = product[:, t * LANES : (t + 1) * LANES]
    for c in range(NCOL):
        for t in range(TILES):
            first = mixed[t, pl.ds(32 * c, CHUNKS, stride=2), :]
            second = mixed[t, pl.ds(32 * c + 1, CHUNKS, stride=2), :]
            even, odd = swap_halves(first, second)
            send[32 * t + c] = even.astype(BF16)
            send[32 * t + 16 + c] = odd.astype(BF16)


def middle_kernel(recv, q_in, gain, bias, send, y_out):
    gain_c = column(gain[...])
    bias_c = column(bias[...])

    def step(s):
        here = lanes_of(s)
        mixed = recv[:, here].astype(F32)
        mean = jnp.mean(mixed, axis=0, keepdims=True)
        centred = mixed - mean
        inverse = lax.rsqrt(jnp.mean(centred * centred, axis=0, keepdims=True) + EPS)
        normed = centred * inverse
        y_out[:, here] = (normed * gain_c + bias_c).astype(BF16)
        q = q_in[:, here]
        first = jnp.mean(q, axis=0, keepdims=True)
        second = jnp.mean(q * normed, axis=0, keepdims=True)
        send[:, here] = ((q - first - normed * second) * inverse).astype(BF16)

    loop(step)


def gate_kernel(
    y, zn_t, slope, grad_update, aux, w_gate, w_out, w_proj,
    terms, half, factor, logit_t, wo_t, wp_t,
):
    wo_t[...] = w_out[...].astype(F32).T.astype(BF16)
    wp_t[...] = w_proj[...].astype(F32).T.astype(BF16)

    def step(s):
        here = lanes_of(s)
        update = dot(wo_t[...], y[:, here], 1, 0)
        grad_logit = (slope[:, here] * update).astype(BF16)
        logit_t[:, here] = grad_logit
        half[:, here] = dot(w_gate[...], grad_logit, 1, 0)
        mask = aux[0:1, here]
        proj = dot(wp_t[...], zn_t[:, here], 1, 0)
        gate_a = sigmoid(proj[:CH])
        gate_b = sigmoid(proj[2 * CH : 3 * CH])
        plain_a = mask * gate_a
        plain_b = mask * gate_b
        factor[0:CH, here] = plain_a * proj[CH : 2 * CH] * (1.0 - gate_a)
        factor[CH : 2 * CH, here] = plain_a
        factor[2 * CH : 3 * CH, here] = plain_b * proj[3 * CH :] * (1.0 - gate_b)
        factor[3 * CH : 4 * CH, here] = plain_b

    loop(step)
    terms[:CH] = dot(y[...], grad_update[...], 1, 1).astype(BF16)
    terms[CH:] = dot(zn_t[...], logit_t[...], 1, 1).astype(BF16)


def unmix_kernel(recv, a_t, b_t, send, strided, grad):
    for c in range(NCOL):
        for t in range(TILES):
            even, odd = swap_halves(
                recv[32 * t + c].astype(F32), recv[32 * t + 16 + c].astype(F32)
            )
            strided[t, pl.ds(32 * c, CHUNKS, stride=2), :] = even
            strided[t, pl.ds(32 * c + 1, CHUNKS, stride=2), :] = odd
    for t in range(TILES):
        grad[:, t * LANES : (t + 1) * LANES] = strided[t].astype(BF16)
    for offset, left, dim in ((0, b_t, 0), (CHUNKS, a_t, 1)):
        product = dot(left[...], grad[...], 1, dim)
        rows = slice(offset, offset + CHUNKS)
        for c in range(NCOL):
            for t in range(TILES):
                spot = slice(t * LANES, (t + 1) * LANES)
                even, odd = swap_halves(
                    product[32 * c : 32 * c + 16, spot], product[32 * c + 16 : 32 * c + 32, spot]
                )
                send[32 * t + c, rows] = even.astype(BF16)
                send[32 * t + 16 + c, rows] = odd.astype(BF16)


def back_kernel(recv, zn_t, factor, terms_in, terms, grad_p):
    def step(s):
        here = lanes_of(s)
        for part in range(4):
            rows = slice(part * CH, (part + 1) * CH)
            grad = recv[:, lanes_of(s, (part // 2) * PAIRS)].astype(F32)
            grad_p[rows, here] = (grad * factor[rows, here]).astype(BF16)

    loop(step)
    product = dot(zn_t[...], grad_p[...], 1, 1)
    for part in range(4):
        terms[part * CH : (part + 1) * CH] = product[:, part * CH : (part + 1) * CH].astype(BF16)
    terms[4 * CH : 6 * CH] = terms_in[...]
    terms[6 * CH :] = jnp.zeros((2 * CH, CH), BF16)


def last_kernel(grad_p, half, normed_t, aux, gain, w_proj, grad_pair, ys):
    gain_c = column(gain[...])

    def step(s):
        here = lanes_of(s)
        grad_zn = dot(w_proj[...], grad_p[:, here], 1, 0) + half[:, here]
        normed = normed_t[:, here]
        q = grad_zn * gain_c
        first = jnp.mean(q, axis=0, keepdims=True)
        second = jnp.mean(q * normed, axis=0, keepdims=True)
        store_chunk(ys, s, (q - first - normed * second) * aux[2:3, here])

    loop(step)
    grad_pair[...] = ys[...].reshape(ROWS, COLS, CH).astype(BF16)


def sum_kernel(parts, out):
    total = jnp.sum(parts[...].astype(F32), axis=0, keepdims=True) * (1.0 / N)
    out[...] = jnp.broadcast_to(total, out.shape).astype(BF16)


def split_kernel(sums, grad_proj, grad_gate, grad_out):
    whole = sums[...].astype(F32).reshape(8 * DEV, LANES)
    for part in range(4):
        grad_proj[:, part * CH : (part + 1) * CH] = whole[part * CH : (part + 1) * CH]
    grad_out[...] = whole[4 * CH : 5 * CH]
    grad_gate[...] = whole[5 * CH : 6 * CH]


def call(kernel, outs, scratch, flops, args, in_hbm=False, vmem=16):
    space = pltpu.HBM if in_hbm else pltpu.VMEM
    moved = sum(x.size * x.dtype.itemsize for x in args) + sum(
        x.size * x.dtype.itemsize for x in outs
    )
    if in_hbm:
        args = [pltpu.with_memory_space_constraint(x, pltpu.HBM) for x in args]
    return pl.pallas_call(
        kernel,
        out_shape=outs,
        in_specs=[pl.BlockSpec(memory_space=space)] * len(args),
        out_specs=[pl.BlockSpec(memory_space=pltpu.VMEM)] * len(outs),
        scratch_shapes=scratch,
        compiler_params=pltpu.CompilerParams(vmem_limit_bytes=vmem << 20),
        cost_estimate=pl.CostEstimate(flops=flops, bytes_accessed=moved, transcendentals=0),
    )(*args)


def exchange(x):
    return lax.all_to_all(x, AXES, 0, 0, tiled=True)


def split_rows(x):
    return x.reshape(DEV, -1, LANES)


def join_rows(x):
    return x.reshape(DEV, -1)


def body(
    pair,
    cotangent,
    res_mask,
    chain,
    ln_in_gain,
    ln_in_bias,
    w_proj,
    w_gate,
    chain_bias,
    ln_out_gain,
    ln_out_bias,
    w_out,
):
    S = jax.ShapeDtypeStruct
    V = pltpu.VMEM
    unit = 2 * PAIRS * CH * CH

    def flat(x):
        return x.reshape(1, -1)

    send_ab, zn_t, normed_t, aux = call(
        front_kernel,
        [S((CH, 2 * PAIRS), BF16), S((CH, PAIRS), BF16), S((CH, PAIRS), F32), S((8, PAIRS), F32)],
        [
            pltpu.SMEM((N,), jnp.int32), pltpu.SMEM((N,), jnp.int32), V((ROWS, COLS, CH), BF16),
            V((1, CH), F32), V((1, CH), F32), V((CH, 4 * CH), BF16),
            V((PAIRS, CH), F32), V((4 * CH, CH), BF16), pltpu.SemaphoreType.DMA((6,)),
        ],
        4 * unit,
        (res_mask, chain, pair, flat(ln_in_gain), flat(ln_in_bias), w_proj),
        in_hbm=True,
    )
    recv_ab = exchange(split_rows(send_ab))
    grad_update, q, slope = call(
        ahead_kernel,
        [S((CH, PAIRS), BF16), S((CH, PAIRS), F32), S((CH, PAIRS), F32)],
        [V((PAIRS, CH), F32), V((CH, CH), BF16)],
        2 * unit,
        (cotangent, zn_t, aux, w_gate, flat(chain_bias), flat(ln_out_gain), w_out),
    )
    recv_ab, grad_update, q, slope = lax.optimization_barrier((recv_ab, grad_update, q, slope))
    send_mixed, a_t, b_t = call(
        mix_kernel,
        [S((DEV, CHUNKS, LANES), BF16), S((N, N), BF16), S((N, N), BF16)],
        [V((TILES, N, LANES), F32)],
        2 * N * N * N,
        (recv_ab,),
    )
    send_grad, y = call(
        middle_kernel,
        [S((CH, PAIRS), BF16), S((CH, PAIRS), BF16)],
        [],
        0,
        (join_rows(exchange(send_mixed)), q, flat(ln_out_gain), flat(ln_out_bias)),
    )
    (send_back,) = call(
        unmix_kernel,
        [S((DEV, 2 * CHUNKS, LANES), BF16)],
        [V((TILES, N, LANES), F32), V((N, N), BF16)],
        4 * N * N * N,
        (exchange(split_rows(send_grad)), a_t, b_t),
    )
    send_back, y, slope = lax.optimization_barrier((send_back, y, slope))
    recv_back = exchange(send_back)
    terms_in, half, factor = call(
        gate_kernel,
        [S((2 * CH, CH), BF16), S((CH, PAIRS), F32), S((4 * CH, PAIRS), F32)],
        [V((CH, PAIRS), BF16), V((CH, CH), BF16), V((4 * CH, CH), BF16)],
        8 * unit,
        (y, zn_t, slope, grad_update, aux, w_gate, w_out, w_proj),
    )
    terms, grad_p = call(
        back_kernel,
        [S((8 * DEV, CH), BF16), S((4 * CH, PAIRS), BF16)],
        [],
        4 * unit,
        (join_rows(recv_back), zn_t, factor, terms_in),
    )
    parts = exchange(split_rows(terms))
    (summed,) = call(sum_kernel, [S((DEV, 8, LANES), BF16)], [], 0, (parts,))
    summed, grad_p, half = lax.optimization_barrier((summed, grad_p, half))
    sums = exchange(summed)
    (grad_pair,) = call(
        last_kernel,
        [S((ROWS, COLS, CH), BF16)],
        [V((PAIRS, CH), F32)],
        4 * unit,
        (grad_p, half, normed_t, aux, flat(ln_in_gain), w_proj),
    )
    grad_proj, grad_gate, grad_out = call(
        split_kernel, [S((CH, 4 * CH), F32), S((CH, CH), F32), S((CH, CH), F32)], [], 0, (sums,)
    )
    return (grad_pair, grad_proj, grad_gate, grad_out)


def solution(mesh):
    return jax.shard_map(
        body,
        mesh=mesh,
        in_specs=(P("row", "col", None), P("row", "col", None)) + (P(),) * 10,
        out_specs=(P("row", "col", None), P(), P(), P()),
        check_vma=False,
    )
```

```python
import functools

import jax
import jax.numpy as jnp
from jax import lax
from jax.experimental import pallas as pl
from jax.experimental.pallas import tpu as pltpu
from jax.sharding import PartitionSpec as P

EPS = 1e-05
F32 = jnp.float32
BF16 = jnp.bfloat16
AXES = ("col", "row")

ROWS = 64
COLS = 32
NROW = 8
NCOL = 16
DEV = NROW * NCOL
CH = 128
N = 512
PAIRS = ROWS * COLS
LANES = 128
CHUNKS = PAIRS // LANES
WIDE = 256
STEPS = PAIRS // WIDE
EACH = WIDE // ROWS
PIECES = 4
TILES = N // LANES


def dot(left, right, dim_left, dim_right):
    return lax.dot_general(
        left, right, (((dim_left,), (dim_right,)), ((), ())), preferred_element_type=F32
    )


def sigmoid(x):
    return 0.5 * jnp.tanh(0.5 * x) + 0.5


def column(row):
    return jnp.broadcast_to(row, (WIDE, row.shape[1])).T


def lanes_of(s, offset=0):
    return pl.ds(pl.multiple_of(s * WIDE + offset, LANES), WIDE)


def swap_halves(first, second):
    low = lax.broadcasted_iota(jnp.int32, first.shape, 1) < LANES // 2
    return (
        jnp.where(low, first, pltpu.roll(second, LANES // 2, 1)),
        jnp.where(low, pltpu.roll(first, LANES // 2, 1), second),
    )


def load_chunk(ref, s):
    parts = [ref[pl.ds(EACH * s + e, ROWS, stride=COLS), :] for e in range(EACH)]
    return jnp.concatenate(parts, axis=0).T


def store_chunk(ref, s, value):
    value = value.T
    for e in range(EACH):
        ref[pl.ds(EACH * s + e, ROWS, stride=COLS), :] = value[e * ROWS : (e + 1) * ROWS]


def loop(step, unroll=2):
    def body(group, carry):
        for u in range(unroll):
            step(group * unroll + u)
        return carry

    lax.fori_loop(0, STEPS // unroll, body, 0)


def front_kernel(
    mask_h, chain_h, pair_h, gain_h, bias_h, w_h,
    send, zn_t, aux,
    mask_s, chain_s, pair, gain, bias, w_proj, xs, w_t, sems,
):
    small = [
        pltpu.make_async_copy(src, dst, sems.at[n])
        for n, (src, dst) in enumerate(
            (
                (w_h, w_proj), (gain_h, gain), (bias_h, bias), (mask_h, mask_s),
                (chain_h, chain_s),
            )
        )
    ]
    pieces = []
    for n in range(PIECES):
        spot = slice(n * COLS // PIECES, (n + 1) * COLS // PIECES)
        pieces.append(pltpu.make_async_copy(pair_h.at[:, spot], pair.at[:, spot], sems.at[5 + n]))
    for copy in small + pieces:
        copy.start()
    for copy in small:
        copy.wait()
    row_start = lax.axis_index("row") * ROWS
    col_start = lax.axis_index("col") * COLS
    w_t[...] = w_proj[...].astype(F32).T.astype(BF16)
    gain_c = column(gain[...])
    bias_c = column(bias[...])
    lane = lax.broadcasted_iota(jnp.int32, (1, LANES), 1)
    place = lane % ROWS
    mask_row = jnp.zeros((1, LANES), jnp.int32)
    chain_row = jnp.zeros((1, LANES), jnp.int32)
    for i in range(ROWS):
        here = place == i
        mask_row = jnp.where(here, mask_s[row_start + i], mask_row)
        chain_row = jnp.where(here, chain_s[row_start + i], chain_row)
    low = lane < ROWS

    def step(s):
        x = load_chunk(xs.reshape(PAIRS, CH), s)
        mean = jnp.mean(x, axis=0, keepdims=True)
        centred = x - mean
        inverse = lax.rsqrt(jnp.mean(centred * centred, axis=0, keepdims=True) + EPS)
        normed = centred * inverse
        zn = (normed * gain_c + bias_c).astype(BF16)
        mask, same = [], []
        for e in range(0, EACH, 2):
            k = col_start + EACH * s + e
            mask.append((jnp.where(low, mask_s[k], mask_s[k + 1]) * mask_row).astype(F32))
            same.append((jnp.where(low, chain_s[k], chain_s[k + 1]) == chain_row).astype(F32))
        mask = jnp.concatenate(mask, axis=1)
        proj = dot(w_t[...], zn, 1, 0)
        act_a = sigmoid(proj[:CH]) * proj[CH : 2 * CH] * mask
        act_b = sigmoid(proj[2 * CH : 3 * CH]) * proj[3 * CH :] * mask
        send[:, lanes_of(s)] = act_a.astype(BF16)
        send[:, lanes_of(s, PAIRS)] = act_b.astype(BF16)
        zn_t[:, lanes_of(s)] = zn
        aux[0:1, lanes_of(s)] = mask
        aux[1:2, lanes_of(s)] = jnp.concatenate(same, axis=1)

    for n in range(PIECES):
        pieces[n].wait()
        spot = slice(n * COLS // PIECES, (n + 1) * COLS // PIECES)
        xs[:, spot] = pair[:, spot].astype(F32)
        for u in range(STEPS // PIECES):
            step(n * (STEPS // PIECES) + u)


def ahead_kernel(
    cot, zn_t, aux, w_gate, chain_bias, gain, w_out, w_proj,
    grad_update, q_out, slope, factor, cs, wg_t, wp_t,
):
    cs[...] = cot[...].astype(F32).reshape(PAIRS, CH)
    wg_t[...] = w_gate[...].astype(F32).T.astype(BF16)
    wp_t[...] = w_proj[...].astype(F32).T.astype(BF16)
    gain_c = column(gain[...])
    chain_c = column(chain_bias[...])

    def step(s):
        here = lanes_of(s)
        zn = zn_t[:, here]
        gate = sigmoid(dot(wg_t[...], zn, 1, 0) + aux[1:2, here] * chain_c)
        gated = load_chunk(cs, s) * gate
        update = gated.astype(BF16)
        grad_update[:, here] = update
        slope[:, here] = gated * (1.0 - gate)
        q_out[:, here] = dot(w_out[...], update, 1, 0) * gain_c
        mask = aux[0:1, here]
        proj = dot(wp_t[...], zn, 1, 0)
        gate_a = sigmoid(proj[:CH])
        gate_b = sigmoid(proj[2 * CH : 3 * CH])
        plain_a = mask * gate_a
        plain_b = mask * gate_b
        factor[0:CH, here] = plain_a * proj[CH : 2 * CH] * (1.0 - gate_a)
        factor[CH : 2 * CH, here] = plain_a
        factor[2 * CH : 3 * CH, here] = plain_b * proj[3 * CH :] * (1.0 - gate_b)
        factor[3 * CH : 4 * CH, here] = plain_b

    loop(step)


def mix_kernel(recv, send, a_t, b_t, mixed):
    for c in range(NCOL):
        for t in range(TILES):
            for offset, out in ((0, a_t), (CHUNKS, b_t)):
                rows = slice(offset, offset + CHUNKS)
                first = recv[8 * c + 2 * t, rows].astype(F32)
                second = recv[8 * c + 2 * t + 1, rows].astype(F32)
                even, odd = swap_halves(first, second)
                spot = slice(t * LANES, (t + 1) * LANES)
                out[32 * c : 32 * c + 16, spot] = even.astype(BF16)
                out[32 * c + 16 : 32 * c + 32, spot] = odd.astype(BF16)
    product = dot(b_t[...], a_t[...], 0, 0)
    for t in range(TILES):
        mixed[t] = product[:, t * LANES : (t + 1) * LANES]
    for c in range(NCOL):
        for t in range(TILES):
            first = mixed[t, pl.ds(32 * c, CHUNKS, stride=2), :]
            second = mixed[t, pl.ds(32 * c + 1, CHUNKS, stride=2), :]
            even, odd = swap_halves(first, second)
            send[8 * c + 2 * t] = even.astype(BF16)
            send[8 * c + 2 * t + 1] = odd.astype(BF16)


def middle_kernel(recv, q_in, gain, bias, send, y_out):
    gain_c = column(gain[...])
    bias_c = column(bias[...])

    def step(s):
        here = lanes_of(s)
        mixed = recv[:, here].astype(F32)
        mean = jnp.mean(mixed, axis=0, keepdims=True)
        centred = mixed - mean
        inverse = lax.rsqrt(jnp.mean(centred * centred, axis=0, keepdims=True) + EPS)
        normed = centred * inverse
        y_out[:, here] = (normed * gain_c + bias_c).astype(BF16)
        q = q_in[:, here]
        first = jnp.mean(q, axis=0, keepdims=True)
        second = jnp.mean(q * normed, axis=0, keepdims=True)
        send[:, here] = ((q - first - normed * second) * inverse).astype(BF16)

    loop(step)


def unmix_kernel(recv, a_t, b_t, send, strided, grad):
    for c in range(NCOL):
        for t in range(TILES):
            even, odd = swap_halves(
                recv[8 * c + 2 * t].astype(F32), recv[8 * c + 2 * t + 1].astype(F32)
            )
            strided[t, pl.ds(32 * c, CHUNKS, stride=2), :] = even
            strided[t, pl.ds(32 * c + 1, CHUNKS, stride=2), :] = odd
    for t in range(TILES):
        grad[:, t * LANES : (t + 1) * LANES] = strided[t].astype(BF16)
    for offset, left, dim in ((0, b_t, 0), (CHUNKS, a_t, 1)):
        product = dot(left[...], grad[...], 1, dim)
        rows = slice(offset, offset + CHUNKS)
        for c in range(NCOL):
            for t in range(TILES):
                spot = slice(t * LANES, (t + 1) * LANES)
                even, odd = swap_halves(
                    product[32 * c : 32 * c + 16, spot], product[32 * c + 16 : 32 * c + 32, spot]
                )
                send[8 * c + 2 * t, rows] = even.astype(BF16)
                send[8 * c + 2 * t + 1, rows] = odd.astype(BF16)


def back_kernel(
    recv, zn_t, factor, y, slope, grad_update, w_out, terms, grad_p, logit_t, wo_t
):
    wo_t[...] = w_out[...].astype(F32).T.astype(BF16)

    def step(s):
        here = lanes_of(s)
        update = dot(wo_t[...], y[:, here], 1, 0)
        logit_t[:, here] = (slope[:, here] * update).astype(BF16)
        for part in range(4):
            rows = slice(part * CH, (part + 1) * CH)
            grad = recv[:, lanes_of(s, (part // 2) * PAIRS)].astype(F32)
            grad_p[rows, here] = (grad * factor[rows, here]).astype(BF16)

    loop(step)
    product = dot(zn_t[...], grad_p[...], 1, 1)
    for part in range(4):
        terms[part * CH : (part + 1) * CH] = product[:, part * CH : (part + 1) * CH].astype(BF16)
    terms[4 * CH : 5 * CH] = dot(y[...], grad_update[...], 1, 1).astype(BF16)
    terms[5 * CH : 6 * CH] = dot(zn_t[...], logit_t[...], 1, 1).astype(BF16)
    terms[6 * CH :] = jnp.zeros((2 * CH, CH), BF16)


def last_kernel(grad_p, logit_t, pair, gain, w_proj, w_gate, grad_pair, xs):
    gain_c = column(gain[...])
    xs[...] = pair[...].astype(F32).reshape(PAIRS, CH)

    def step(s):
        here = lanes_of(s)
        grad_zn = dot(w_proj[...], grad_p[:, here], 1, 0) + dot(w_gate[...], logit_t[:, here], 1, 0)
        x = load_chunk(xs, s)
        centred = x - jnp.mean(x, axis=0, keepdims=True)
        inverse = lax.rsqrt(jnp.mean(centred * centred, axis=0, keepdims=True) + EPS)
        normed = centred * inverse
        q = grad_zn * gain_c
        first = jnp.mean(q, axis=0, keepdims=True)
        second = jnp.mean(q * normed, axis=0, keepdims=True)
        store_chunk(xs, s, (q - first - normed * second) * inverse)

    loop(step)
    grad_pair[...] = xs[...].reshape(ROWS, COLS, CH).astype(BF16)


def sum_kernel(parts, out):
    total = jnp.sum(parts[...].astype(F32), axis=0, keepdims=True) * (1.0 / N)
    out[...] = jnp.broadcast_to(total, out.shape).astype(BF16)


def split_kernel(sums, grad_proj, grad_gate, grad_out):
    whole = sums[...].astype(F32).reshape(8 * DEV, LANES)
    for part in range(4):
        grad_proj[:, part * CH : (part + 1) * CH] = whole[part * CH : (part + 1) * CH]
    grad_out[...] = whole[4 * CH : 5 * CH]
    grad_gate[...] = whole[5 * CH : 6 * CH]


def call(kernel, outs, scratch, flops, args, in_hbm=False, vmem=16):
    space = pltpu.HBM if in_hbm else pltpu.VMEM
    moved = sum(x.size * x.dtype.itemsize for x in args) + sum(
        x.size * x.dtype.itemsize for x in outs
    )
    if in_hbm:
        args = [pltpu.with_memory_space_constraint(x, pltpu.HBM) for x in args]
    return pl.pallas_call(
        kernel,
        out_shape=outs,
        in_specs=[pl.BlockSpec(memory_space=space)] * len(args),
        out_specs=[pl.BlockSpec(memory_space=pltpu.VMEM)] * len(outs),
        scratch_shapes=scratch,
        compiler_params=pltpu.CompilerParams(vmem_limit_bytes=vmem << 20),
        cost_estimate=pl.CostEstimate(flops=flops, bytes_accessed=moved, transcendentals=0),
    )(*args)


def exchange(x):
    return lax.all_to_all(x, AXES, 0, 0, tiled=True)


def split_rows(x):
    return x.reshape(DEV, -1, LANES)


def join_rows(x):
    return x.reshape(DEV, -1)


def body(
    pair,
    cotangent,
    res_mask,
    chain,
    ln_in_gain,
    ln_in_bias,
    w_proj,
    w_gate,
    chain_bias,
    ln_out_gain,
    ln_out_bias,
    w_out,
):
    S = jax.ShapeDtypeStruct
    V = pltpu.VMEM
    unit = 2 * PAIRS * CH * CH

    def flat(x):
        return x.reshape(1, -1)

    send_ab, zn_t, aux = call(
        front_kernel,
        [S((CH, 2 * PAIRS), BF16), S((CH, PAIRS), BF16), S((8, PAIRS), F32)],
        [
            pltpu.SMEM((N,), jnp.int32), pltpu.SMEM((N,), jnp.int32), V((ROWS, COLS, CH), BF16),
            V((1, CH), F32), V((1, CH), F32), V((CH, 4 * CH), BF16),
            V((ROWS, COLS, CH), F32), V((4 * CH, CH), BF16),
            pltpu.SemaphoreType.DMA((5 + PIECES,)),
        ],
        4 * unit,
        (res_mask, chain, pair, flat(ln_in_gain), flat(ln_in_bias), w_proj),
        in_hbm=True,
    )
    recv_ab = exchange(split_rows(send_ab))
    grad_update, q, slope, factor = call(
        ahead_kernel,
        [
            S((CH, PAIRS), BF16), S((CH, PAIRS), F32), S((CH, PAIRS), F32),
            S((4 * CH, PAIRS), F32),
        ],
        [V((PAIRS, CH), F32), V((CH, CH), BF16), V((4 * CH, CH), BF16)],
        6 * unit,
        (cotangent, zn_t, aux, w_gate, flat(chain_bias), flat(ln_out_gain), w_out, w_proj),
    )
    recv_ab, grad_update, q, slope, factor = lax.optimization_barrier(
        (recv_ab, grad_update, q, slope, factor)
    )
    send_mixed, a_t, b_t = call(
        mix_kernel,
        [S((DEV, CHUNKS, LANES), BF16), S((N, N), BF16), S((N, N), BF16)],
        [V((TILES, N, LANES), F32)],
        2 * N * N * N,
        (recv_ab,),
    )
    send_grad, y = call(
        middle_kernel,
        [S((CH, PAIRS), BF16), S((CH, PAIRS), BF16)],
        [],
        0,
        (join_rows(exchange(send_mixed)), q, flat(ln_out_gain), flat(ln_out_bias)),
    )
    (send_back,) = call(
        unmix_kernel,
        [S((DEV, 2 * CHUNKS, LANES), BF16)],
        [V((TILES, N, LANES), F32), V((N, N), BF16)],
        4 * N * N * N,
        (exchange(split_rows(send_grad)), a_t, b_t),
    )
    terms, grad_p, logit_t = call(
        back_kernel,
        [S((8 * DEV, CH), BF16), S((4 * CH, PAIRS), BF16), S((CH, PAIRS), BF16)],
        [V((CH, CH), BF16)],
        7 * unit,
        (join_rows(exchange(send_back)), zn_t, factor, y, slope, grad_update, w_out),
    )
    parts = exchange(split_rows(terms))
    (summed,) = call(sum_kernel, [S((DEV, 8, LANES), BF16)], [], 0, (parts,))
    summed, grad_p, logit_t = lax.optimization_barrier((summed, grad_p, logit_t))
    sums = exchange(summed)
    (grad_pair,) = call(
        last_kernel,
        [S((ROWS, COLS, CH), BF16)],
        [V((PAIRS, CH), F32)],
        5 * unit,
        (grad_p, logit_t, pair, flat(ln_in_gain), w_proj, w_gate),
    )
    grad_proj, grad_gate, grad_out = call(
        split_kernel, [S((CH, 4 * CH), F32), S((CH, CH), F32), S((CH, CH), F32)], [], 0, (sums,)
    )
    return (grad_pair, grad_proj, grad_gate, grad_out)


def solution(mesh):
    return jax.shard_map(
        body,
        mesh=mesh,
        in_specs=(P("row", "col", None), P("row", "col", None)) + (P(),) * 10,
        out_specs=(P("row", "col", None), P(), P(), P()),
        check_vma=False,
    )
```

```python
import functools

import jax
import jax.numpy as jnp
from jax import lax
from jax.experimental import pallas as pl
from jax.experimental.pallas import tpu as pltpu
from jax.sharding import PartitionSpec as P

EPS = 1e-05
F32 = jnp.float32
BF16 = jnp.bfloat16
AXES = ("col", "row")

ROWS = 64
COLS = 32
NROW = 8
NCOL = 16
DEV = NROW * NCOL
CH = 128
N = 512
PAIRS = ROWS * COLS
LANES = 128
CHUNKS = PAIRS // LANES
WIDE = 256
STEPS = PAIRS // WIDE
EACH = WIDE // ROWS
PIECES = 2
TILES = N // LANES


def dot(left, right, dim_left, dim_right):
    return lax.dot_general(
        left, right, (((dim_left,), (dim_right,)), ((), ())), preferred_element_type=F32
    )


def column(row):
    return jnp.broadcast_to(row, (WIDE, row.shape[1])).T


def lanes_of(s, offset=0):
    return slice(offset + s * WIDE, offset + (s + 1) * WIDE)


def swap_halves(first, second):
    low = lax.broadcasted_iota(jnp.int32, first.shape, 1) < LANES // 2
    return (
        jnp.where(low, first, pltpu.roll(second, LANES // 2, 1)),
        jnp.where(low, pltpu.roll(first, LANES // 2, 1), second),
    )


def load_chunk(ref, s):
    parts = [ref[pl.ds(EACH * s + e, ROWS, stride=COLS), :] for e in range(EACH)]
    return jnp.concatenate(parts, axis=0).astype(BF16).T.astype(F32)


def store_chunk(ref, s, value):
    value = value.astype(BF16).T.astype(F32)
    for e in range(EACH):
        ref[pl.ds(EACH * s + e, ROWS, stride=COLS), :] = value[e * ROWS : (e + 1) * ROWS]


def loop(step):
    for s in range(STEPS):
        step(s)


def front_kernel(
    mask_h, chain_h, gain_h, bias_h, chain_bias_h, out_gain_h, w_proj_h, w_gate_h, w_out_h,
    pair_h, cot_h,
    send, zn_t, grad_update, q_out, slope, factor,
    mask_s, chain_s, gain, bias, chain_bias, out_gain, w_proj, w_gate, w_out, pair, cot,
    xs, cs, wp_t, wg_t, sems,
):
    small = [
        pltpu.make_async_copy(src, dst, sems.at[n])
        for n, (src, dst) in enumerate(
            (
                (mask_h, mask_s), (chain_h, chain_s), (gain_h, gain), (bias_h, bias),
                (chain_bias_h, chain_bias), (out_gain_h, out_gain), (w_proj_h, w_proj),
                (w_gate_h, w_gate), (w_out_h, w_out),
            )
        )
    ]
    pieces = []
    for n in range(PIECES):
        spot = slice(n * COLS // PIECES, (n + 1) * COLS // PIECES)
        for m, (src, dst) in enumerate(((pair_h, pair), (cot_h, cot))):
            pieces.append(
                pltpu.make_async_copy(src.at[:, spot], dst.at[:, spot], sems.at[9 + 2 * n + m])
            )
    for copy in small + pieces:
        copy.start()
    for copy in small:
        copy.wait()
    columns = jnp.concatenate(
        [gain[...], bias[...], 0.5 * chain_bias[...], out_gain[...], jnp.zeros((4, CH), F32)], axis=0
    ).T
    gain_c, bias_c, chain_c, out_gain_c = (
        jnp.broadcast_to(columns[:, n : n + 1], (CH, WIDE)) for n in range(4)
    )
    row_start = lax.axis_index("row") * ROWS
    col_start = lax.axis_index("col") * COLS
    for n in range(4):
        weights = w_proj[:, n * CH : (n + 1) * CH].astype(F32).T
        wp_t[n * CH : (n + 1) * CH] = (weights if n % 2 else 0.5 * weights).astype(BF16)
    wg_t[...] = (0.5 * w_gate[...].astype(F32).T).astype(BF16)
    lane = lax.broadcasted_iota(jnp.int32, (1, LANES), 1)
    place = lane % ROWS
    mask_row = jnp.zeros((1, LANES), jnp.int32)
    chain_row = jnp.zeros((1, LANES), jnp.int32)
    for i in range(ROWS):
        here = place == i
        mask_row = jnp.where(here, mask_s[row_start + i], mask_row)
        chain_row = jnp.where(here, chain_s[row_start + i], chain_row)
    low = lane < ROWS

    def step(s):
        here = lanes_of(s)
        x = load_chunk(xs.reshape(PAIRS, CH), s)
        mean = jnp.mean(x, axis=0, keepdims=True)
        centred = x - mean
        inverse = lax.rsqrt(jnp.mean(centred * centred, axis=0, keepdims=True) + EPS)
        zn = (centred * inverse * gain_c + bias_c).astype(BF16)
        zn_t[:, here] = zn
        mask, same = [], []
        for e in range(0, EACH, 2):
            k = col_start + EACH * s + e
            mask.append((jnp.where(low, mask_s[k], mask_s[k + 1]) * mask_row).astype(F32))
            same.append((jnp.where(low, chain_s[k], chain_s[k + 1]) == chain_row).astype(F32))
        half = 0.5 * jnp.concatenate(mask, axis=1)
        same = jnp.concatenate(same, axis=1)
        proj = dot(wp_t[...], zn, 1, 0)
        for side in range(2):
            base = 2 * CH * side
            plain = jnp.tanh(proj[base : base + CH]) * half + half
            act = plain * proj[base + CH : base + 2 * CH]
            send[:, lanes_of(s, side * PAIRS)] = act.astype(BF16)
            factor[base : base + CH, here] = (act - act * plain).astype(BF16)
            factor[base + CH : base + 2 * CH, here] = plain.astype(BF16)
        gate = 0.5 * jnp.tanh(dot(wg_t[...], zn, 1, 0) + same * chain_c) + 0.5
        gated = load_chunk(cs.reshape(PAIRS, CH), s) * gate
        update = gated.astype(BF16)
        grad_update[:, here] = update
        slope[:, here] = gated - gated * gate
        q_out[:, here] = dot(w_out[...], update, 1, 0) * out_gain_c

    for n in range(PIECES):
        pieces[2 * n].wait()
        pieces[2 * n + 1].wait()
        spot = slice(n * COLS // PIECES, (n + 1) * COLS // PIECES)
        xs[:, spot] = pair[:, spot].astype(F32)
        cs[:, spot] = cot[:, spot].astype(F32)
        for u in range(STEPS // PIECES):
            step(n * (STEPS // PIECES) + u)


def mix_kernel(recv, send, a_t, b_t, mixed):
    for c in range(NCOL):
        for t in range(TILES):
            for offset, out in ((0, a_t), (CHUNKS, b_t)):
                rows = slice(offset, offset + CHUNKS)
                first = recv[8 * c + 2 * t, rows].astype(F32)
                second = recv[8 * c + 2 * t + 1, rows].astype(F32)
                even, odd = swap_halves(first, second)
                spot = slice(t * LANES, (t + 1) * LANES)
                out[32 * c : 32 * c + 16, spot] = even.astype(BF16)
                out[32 * c + 16 : 32 * c + 32, spot] = odd.astype(BF16)
    product = dot(b_t[...], a_t[...], 0, 0)
    for t in range(TILES):
        mixed[t] = product[:, t * LANES : (t + 1) * LANES]
    for c in range(NCOL):
        for t in range(TILES):
            first = mixed[t, pl.ds(32 * c, CHUNKS, stride=2), :]
            second = mixed[t, pl.ds(32 * c + 1, CHUNKS, stride=2), :]
            even, odd = swap_halves(first, second)
            send[8 * c + 2 * t] = even.astype(BF16)
            send[8 * c + 2 * t + 1] = odd.astype(BF16)


def middle_kernel(recv, q_in, gain, bias, send, y_out):
    gain_c = column(gain[...])
    bias_c = column(bias[...])

    def step(s):
        here = lanes_of(s)
        mixed = recv[:, here].astype(F32)
        mean = jnp.mean(mixed, axis=0, keepdims=True)
        centred = mixed - mean
        inverse = lax.rsqrt(jnp.mean(centred * centred, axis=0, keepdims=True) + EPS)
        normed = centred * inverse
        y_out[:, here] = (normed * gain_c + bias_c).astype(BF16)
        q = q_in[:, here]
        first = jnp.mean(q, axis=0, keepdims=True)
        second = jnp.mean(q * normed, axis=0, keepdims=True)
        send[:, here] = ((q - first - normed * second) * inverse).astype(BF16)

    loop(step)


def unmix_kernel(recv, a_t, b_t, send, strided, grad):
    for c in range(NCOL):
        for t in range(TILES):
            even, odd = swap_halves(
                recv[8 * c + 2 * t].astype(F32), recv[8 * c + 2 * t + 1].astype(F32)
            )
            strided[t, pl.ds(32 * c, CHUNKS, stride=2), :] = even
            strided[t, pl.ds(32 * c + 1, CHUNKS, stride=2), :] = odd
    for t in range(TILES):
        grad[:, t * LANES : (t + 1) * LANES] = strided[t].astype(BF16)
    for offset, left, dim in ((0, b_t, 0), (CHUNKS, a_t, 1)):
        product = dot(left[...], grad[...], 1, dim)
        rows = slice(offset, offset + CHUNKS)
        for c in range(NCOL):
            for t in range(TILES):
                spot = slice(t * LANES, (t + 1) * LANES)
                even, odd = swap_halves(
                    product[32 * c : 32 * c + 16, spot], product[32 * c + 16 : 32 * c + 32, spot]
                )
                send[8 * c + 2 * t, rows] = even.astype(BF16)
                send[8 * c + 2 * t + 1, rows] = odd.astype(BF16)


def back_kernel(
    recv, zn_t, factor, y, slope, grad_update, w_out, terms, grad_p, logit_t, wo_t
):
    wo_t[...] = w_out[...].astype(F32).T.astype(BF16)

    def step(s):
        here = lanes_of(s)
        update = dot(wo_t[...], y[:, here], 1, 0)
        logit_t[:, here] = (slope[:, here] * update).astype(BF16)
        for part in range(4):
            rows = slice(part * CH, (part + 1) * CH)
            grad_p[rows, here] = recv[:, lanes_of(s, (part // 2) * PAIRS)] * factor[rows, here]

    loop(step)
    zn = zn_t[...].T
    terms[: 4 * CH] = dot(grad_p[...], zn, 1, 0).astype(BF16)
    terms[4 * CH : 5 * CH] = dot(logit_t[...], zn, 1, 0).astype(BF16)
    terms[5 * CH : 6 * CH] = dot(y[...], grad_update[...], 1, 1).astype(BF16)
    terms[6 * CH :] = jnp.zeros((2 * CH, CH), BF16)


def last_kernel(grad_p, logit_t, pair, gain, w_proj, w_gate, grad_pair, xs):
    gain_c = column(gain[...])
    xs[...] = pair[...].astype(F32).reshape(PAIRS, CH)

    def step(s):
        here = lanes_of(s)
        grad_zn = dot(w_proj[...], grad_p[:, here], 1, 0) + dot(w_gate[...], logit_t[:, here], 1, 0)
        x = load_chunk(xs, s)
        centred = x - jnp.mean(x, axis=0, keepdims=True)
        inverse = lax.rsqrt(jnp.mean(centred * centred, axis=0, keepdims=True) + EPS)
        normed = centred * inverse
        q = grad_zn * gain_c
        first = jnp.mean(q, axis=0, keepdims=True)
        second = jnp.mean(q * normed, axis=0, keepdims=True)
        store_chunk(xs, s, (q - first - normed * second) * inverse)

    loop(step)
    grad_pair[...] = xs[...].reshape(ROWS, COLS, CH).astype(BF16)


def sum_kernel(parts, out):
    total = parts[...].astype(F32)
    while total.shape[0] > 1:
        half = total.shape[0] // 2
        total = total[:half] + total[half:]
    out[...] = jnp.broadcast_to(total * (1.0 / N), out.shape).astype(BF16)


def split_kernel(sums, grad_proj, grad_gate, grad_out):
    whole = sums[...].astype(F32).reshape(8 * DEV, LANES)
    for part in range(4):
        grad_proj[:, part * CH : (part + 1) * CH] = whole[part * CH : (part + 1) * CH].T
    grad_gate[...] = whole[4 * CH : 5 * CH].T
    grad_out[...] = whole[5 * CH : 6 * CH]


def call(kernel, outs, scratch, flops, args, in_hbm=False, vmem=16):
    space = pltpu.HBM if in_hbm else pltpu.VMEM
    moved = sum(x.size * x.dtype.itemsize for x in args) + sum(
        x.size * x.dtype.itemsize for x in outs
    )
    if in_hbm:
        args = [pltpu.with_memory_space_constraint(x, pltpu.HBM) for x in args]
    return pl.pallas_call(
        kernel,
        out_shape=outs,
        in_specs=[pl.BlockSpec(memory_space=space)] * len(args),
        out_specs=[pl.BlockSpec(memory_space=pltpu.VMEM)] * len(outs),
        scratch_shapes=scratch,
        compiler_params=pltpu.CompilerParams(vmem_limit_bytes=vmem << 20),
        cost_estimate=pl.CostEstimate(flops=flops, bytes_accessed=moved, transcendentals=0),
    )(*args)


def exchange(x):
    return lax.all_to_all(x, AXES, 0, 0, tiled=True)


def split_rows(x):
    return x.reshape(DEV, -1, LANES)


def join_rows(x):
    return x.reshape(DEV, -1)


def body(
    pair,
    cotangent,
    res_mask,
    chain,
    ln_in_gain,
    ln_in_bias,
    w_proj,
    w_gate,
    chain_bias,
    ln_out_gain,
    ln_out_bias,
    w_out,
):
    S = jax.ShapeDtypeStruct
    V = pltpu.VMEM
    unit = 2 * PAIRS * CH * CH

    def flat(x):
        return x.reshape(1, -1)

    send_ab, zn_t, grad_update, q, slope, factor = call(
        front_kernel,
        [
            S((CH, 2 * PAIRS), BF16), S((CH, PAIRS), BF16), S((CH, PAIRS), BF16),
            S((CH, PAIRS), F32), S((CH, PAIRS), F32), S((4 * CH, PAIRS), BF16),
        ],
        [
            pltpu.SMEM((N,), jnp.int32), pltpu.SMEM((N,), jnp.int32),
            V((1, CH), F32), V((1, CH), F32), V((1, CH), F32), V((1, CH), F32),
            V((CH, 4 * CH), BF16), V((CH, CH), BF16), V((CH, CH), BF16),
            V((ROWS, COLS, CH), BF16), V((ROWS, COLS, CH), BF16),
            V((ROWS, COLS, CH), F32), V((ROWS, COLS, CH), F32),
            V((4 * CH, CH), BF16), V((CH, CH), BF16),
            pltpu.SemaphoreType.DMA((9 + 2 * PIECES,)),
        ],
        6 * unit,
        (
            res_mask, chain, flat(ln_in_gain), flat(ln_in_bias), flat(chain_bias),
            flat(ln_out_gain), w_proj, w_gate, w_out, pair, cotangent,
        ),
        in_hbm=True,
    )
    recv_ab = exchange(split_rows(send_ab))
    send_mixed, a_t, b_t = call(
        mix_kernel,
        [S((DEV, CHUNKS, LANES), BF16), S((N, N), BF16), S((N, N), BF16)],
        [V((TILES, N, LANES), F32)],
        2 * N * N * N,
        (recv_ab,),
    )
    send_grad, y = call(
        middle_kernel,
        [S((CH, PAIRS), BF16), S((CH, PAIRS), BF16)],
        [],
        0,
        (join_rows(exchange(send_mixed)), q, flat(ln_out_gain), flat(ln_out_bias)),
    )
    (send_back,) = call(
        unmix_kernel,
        [S((DEV, 2 * CHUNKS, LANES), BF16)],
        [V((TILES, N, LANES), F32), V((N, N), BF16)],
        4 * N * N * N,
        (exchange(split_rows(send_grad)), a_t, b_t),
    )
    terms, grad_p, logit_t = call(
        back_kernel,
        [S((8 * DEV, CH), BF16), S((4 * CH, PAIRS), BF16), S((CH, PAIRS), BF16)],
        [V((CH, CH), BF16)],
        7 * unit,
        (join_rows(exchange(send_back)), zn_t, factor, y, slope, grad_update, w_out),
    )
    parts = exchange(split_rows(terms))
    (summed,) = call(sum_kernel, [S((DEV, 8, LANES), BF16)], [], 0, (parts,))
    summed, grad_p, logit_t = lax.optimization_barrier((summed, grad_p, logit_t))
    sums = exchange(summed)
    (grad_pair,) = call(
        last_kernel,
        [S((ROWS, COLS, CH), BF16)],
        [V((PAIRS, CH), F32)],
        5 * unit,
        (grad_p, logit_t, pair, flat(ln_in_gain), w_proj, w_gate),
    )
    grad_proj, grad_gate, grad_out = call(
        split_kernel, [S((CH, 4 * CH), F32), S((CH, CH), F32), S((CH, CH), F32)], [], 0, (sums,)
    )
    return (grad_pair, grad_proj, grad_gate, grad_out)


def solution(mesh):
    return jax.shard_map(
        body,
        mesh=mesh,
        in_specs=(P("row", "col", None), P("row", "col", None)) + (P(),) * 10,
        out_specs=(P("row", "col", None), P(), P(), P()),
        check_vma=False,
    )
```

```python
import functools

import jax
import jax.numpy as jnp
from jax import lax
from jax.experimental import pallas as pl
from jax.experimental.pallas import tpu as pltpu
from jax.sharding import PartitionSpec as P

EPS = 1e-05
F32 = jnp.float32
BF16 = jnp.bfloat16
AXES = ("col", "row")

ROWS = 64
COLS = 32
NROW = 8
NCOL = 16
DEV = NROW * NCOL
CH = 128
N = 512
PAIRS = ROWS * COLS
LANES = 128
CHUNKS = PAIRS // LANES
WIDE = 256
STEPS = PAIRS // WIDE
EACH = WIDE // ROWS
PIECES = 2
TILES = N // LANES
SHARE = 6 * CH // DEV


def dot(left, right, dim_left, dim_right):
    return lax.dot_general(
        left, right, (((dim_left,), (dim_right,)), ((), ())), preferred_element_type=F32
    )


def column(row):
    return jnp.broadcast_to(row, (WIDE, row.shape[1])).T


def lanes_of(s, offset=0):
    return slice(offset + s * WIDE, offset + (s + 1) * WIDE)


def swap_halves(first, second):
    low = lax.broadcasted_iota(jnp.int32, first.shape, 1) < LANES // 2
    return (
        jnp.where(low, first, pltpu.roll(second, LANES // 2, 1)),
        jnp.where(low, pltpu.roll(first, LANES // 2, 1), second),
    )


def load_chunk(ref, s):
    parts = [ref[pl.ds(EACH * s + e, ROWS, stride=COLS), :] for e in range(EACH)]
    return jnp.concatenate(parts, axis=0).astype(BF16).T.astype(F32)


def store_chunk(ref, s, value):
    value = value.astype(BF16).T.astype(F32)
    for e in range(EACH):
        ref[pl.ds(EACH * s + e, ROWS, stride=COLS), :] = value[e * ROWS : (e + 1) * ROWS]


def loop(step):
    for s in range(STEPS):
        step(s)


def front_kernel(
    mask_h, chain_h, gain_h, bias_h, chain_bias_h, out_gain_h, w_proj_h, w_gate_h, w_out_h,
    pair_h, cot_h,
    send, zn_t, grad_update, q_out, slope, factor,
    mask_s, chain_s, gain, bias, chain_bias, out_gain, w_proj, w_gate, w_out, pair, cot,
    xs, cs, wp_t, wg_t, sems,
):
    small = [
        pltpu.make_async_copy(src, dst, sems.at[n])
        for n, (src, dst) in enumerate(
            (
                (mask_h, mask_s), (chain_h, chain_s), (gain_h, gain), (bias_h, bias),
                (chain_bias_h, chain_bias), (out_gain_h, out_gain), (w_proj_h, w_proj),
                (w_gate_h, w_gate), (w_out_h, w_out),
            )
        )
    ]
    pieces = []
    for n in range(PIECES):
        spot = slice(n * COLS // PIECES, (n + 1) * COLS // PIECES)
        for m, (src, dst) in enumerate(((pair_h, pair), (cot_h, cot))):
            pieces.append(
                pltpu.make_async_copy(src.at[:, spot], dst.at[:, spot], sems.at[9 + 2 * n + m])
            )
    for copy in small + pieces:
        copy.start()
    for copy in small:
        copy.wait()
    columns = jnp.concatenate(
        [gain[...], bias[...], 0.5 * chain_bias[...], out_gain[...], jnp.zeros((4, CH), F32)], axis=0
    ).T
    gain_c, bias_c, chain_c, out_gain_c = (
        jnp.broadcast_to(columns[:, n : n + 1], (CH, WIDE)) for n in range(4)
    )
    row_start = lax.axis_index("row") * ROWS
    col_start = lax.axis_index("col") * COLS
    for n in range(4):
        weights = w_proj[:, n * CH : (n + 1) * CH].astype(F32).T
        wp_t[n * CH : (n + 1) * CH] = (weights if n % 2 else 0.5 * weights).astype(BF16)
    wg_t[...] = (0.5 * w_gate[...].astype(F32).T).astype(BF16)
    lane = lax.broadcasted_iota(jnp.int32, (1, LANES), 1)
    place = lane % ROWS
    mask_row = jnp.zeros((1, LANES), jnp.int32)
    chain_row = jnp.zeros((1, LANES), jnp.int32)
    for i in range(ROWS):
        here = place == i
        mask_row = jnp.where(here, mask_s[row_start + i], mask_row)
        chain_row = jnp.where(here, chain_s[row_start + i], chain_row)
    low = lane < ROWS

    def step(s):
        here = lanes_of(s)
        x = load_chunk(xs.reshape(PAIRS, CH), s)
        mean = jnp.mean(x, axis=0, keepdims=True)
        centred = x - mean
        inverse = lax.rsqrt(jnp.mean(centred * centred, axis=0, keepdims=True) + EPS)
        zn = (centred * inverse * gain_c + bias_c).astype(BF16)
        zn_t[:, here] = zn
        mask, same = [], []
        for e in range(0, EACH, 2):
            k = col_start + EACH * s + e
            mask.append((jnp.where(low, mask_s[k], mask_s[k + 1]) * mask_row).astype(F32))
            same.append((jnp.where(low, chain_s[k], chain_s[k + 1]) == chain_row).astype(F32))
        half = 0.5 * jnp.concatenate(mask, axis=1)
        same = jnp.concatenate(same, axis=1)
        proj = dot(wp_t[...], zn, 1, 0)
        for side in range(2):
            base = 2 * CH * side
            plain = jnp.tanh(proj[base : base + CH]) * half + half
            act = plain * proj[base + CH : base + 2 * CH]
            send[:, lanes_of(s, side * PAIRS)] = act.astype(BF16)
            factor[base : base + CH, here] = (act - act * plain).astype(BF16)
            factor[base + CH : base + 2 * CH, here] = plain.astype(BF16)
        gate = 0.5 * jnp.tanh(dot(wg_t[...], zn, 1, 0) + same * chain_c) + 0.5
        gated = load_chunk(cs.reshape(PAIRS, CH), s) * gate
        update = gated.astype(BF16)
        grad_update[:, here] = update
        slope[:, here] = gated - gated * gate
        q_out[:, here] = dot(w_out[...], update, 1, 0) * out_gain_c

    for n in range(PIECES):
        pieces[2 * n].wait()
        pieces[2 * n + 1].wait()
        spot = slice(n * COLS // PIECES, (n + 1) * COLS // PIECES)
        xs[:, spot] = pair[:, spot].astype(F32)
        cs[:, spot] = cot[:, spot].astype(F32)
        for u in range(STEPS // PIECES):
            step(n * (STEPS // PIECES) + u)


def mix_kernel(recv, send, a_t, b_t, mixed):
    for c in range(NCOL):
        for t in range(TILES):
            for offset, out in ((0, a_t), (CHUNKS, b_t)):
                rows = slice(offset, offset + CHUNKS)
                first = recv[8 * c + 2 * t, rows].astype(F32)
                second = recv[8 * c + 2 * t + 1, rows].astype(F32)
                even, odd = swap_halves(first, second)
                spot = slice(t * LANES, (t + 1) * LANES)
                out[32 * c : 32 * c + 16, spot] = even.astype(BF16)
                out[32 * c + 16 : 32 * c + 32, spot] = odd.astype(BF16)
    product = dot(b_t[...], a_t[...], 0, 0)
    for t in range(TILES):
        mixed[t] = product[:, t * LANES : (t + 1) * LANES]
    for c in range(NCOL):
        for t in range(TILES):
            first = mixed[t, pl.ds(32 * c, CHUNKS, stride=2), :]
            second = mixed[t, pl.ds(32 * c + 1, CHUNKS, stride=2), :]
            even, odd = swap_halves(first, second)
            send[8 * c + 2 * t] = even.astype(BF16)
            send[8 * c + 2 * t + 1] = odd.astype(BF16)


def middle_kernel(recv, q_in, gain, bias, send, y_out):
    gain_c = column(gain[...])
    bias_c = column(bias[...])

    def step(s):
        here = lanes_of(s)
        mixed = recv[:, here].astype(F32)
        mean = jnp.mean(mixed, axis=0, keepdims=True)
        centred = mixed - mean
        inverse = lax.rsqrt(jnp.mean(centred * centred, axis=0, keepdims=True) + EPS)
        normed = centred * inverse
        y_out[:, here] = (normed * gain_c + bias_c).astype(BF16)
        q = q_in[:, here]
        first = jnp.mean(q, axis=0, keepdims=True)
        second = jnp.mean(q * normed, axis=0, keepdims=True)
        send[:, here] = ((q - first - normed * second) * inverse).astype(BF16)

    loop(step)


def unmix_kernel(recv, a_t, b_t, send, strided, grad):
    for c in range(NCOL):
        for t in range(TILES):
            even, odd = swap_halves(
                recv[8 * c + 2 * t].astype(F32), recv[8 * c + 2 * t + 1].astype(F32)
            )
            strided[t, pl.ds(32 * c, CHUNKS, stride=2), :] = even
            strided[t, pl.ds(32 * c + 1, CHUNKS, stride=2), :] = odd
    for t in range(TILES):
        grad[:, t * LANES : (t + 1) * LANES] = strided[t].astype(BF16)
    for offset, left, dim in ((0, b_t, 0), (CHUNKS, a_t, 1)):
        product = dot(left[...], grad[...], 1, dim)
        rows = slice(offset, offset + CHUNKS)
        for c in range(NCOL):
            for t in range(TILES):
                spot = slice(t * LANES, (t + 1) * LANES)
                even, odd = swap_halves(
                    product[32 * c : 32 * c + 16, spot], product[32 * c + 16 : 32 * c + 32, spot]
                )
                send[8 * c + 2 * t, rows] = even.astype(BF16)
                send[8 * c + 2 * t + 1, rows] = odd.astype(BF16)


def back_kernel(
    recv, zn_t, factor, y, slope, grad_update, w_out, terms, grad_p, logit_t, wo_t
):
    wo_t[...] = w_out[...].astype(F32).T.astype(BF16)

    def step(s):
        here = lanes_of(s)
        update = dot(wo_t[...], y[:, here], 1, 0)
        logit_t[:, here] = (slope[:, here] * update).astype(BF16)
        for part in range(4):
            rows = slice(part * CH, (part + 1) * CH)
            grad_p[rows, here] = recv[:, lanes_of(s, (part // 2) * PAIRS)] * factor[rows, here]

    loop(step)
    zn = zn_t[...].T
    terms[: 4 * CH] = dot(grad_p[...], zn, 1, 0).astype(BF16)
    terms[4 * CH : 5 * CH] = dot(logit_t[...], zn, 1, 0).astype(BF16)
    terms[5 * CH :] = dot(y[...], grad_update[...], 1, 1).astype(BF16)


def last_kernel(grad_p, logit_t, pair, gain, w_proj, w_gate, grad_pair, xs):
    gain_c = column(gain[...])
    xs[...] = pair[...].astype(F32).reshape(PAIRS, CH)

    def step(s):
        here = lanes_of(s)
        grad_zn = dot(w_proj[...], grad_p[:, here], 1, 0) + dot(w_gate[...], logit_t[:, here], 1, 0)
        x = load_chunk(xs, s)
        centred = x - jnp.mean(x, axis=0, keepdims=True)
        inverse = lax.rsqrt(jnp.mean(centred * centred, axis=0, keepdims=True) + EPS)
        normed = centred * inverse
        q = grad_zn * gain_c
        first = jnp.mean(q, axis=0, keepdims=True)
        second = jnp.mean(q * normed, axis=0, keepdims=True)
        store_chunk(xs, s, (q - first - normed * second) * inverse)

    loop(step)
    grad_pair[...] = xs[...].reshape(ROWS, COLS, CH).astype(BF16)


def sum_kernel(parts, out):
    total = parts[...].astype(F32).reshape(DEV // 4, 4 * SHARE, LANES)
    while total.shape[0] > 1:
        half = total.shape[0] // 2
        total = total[:half] + total[half:]
    total = total[0]
    mine = total[:SHARE]
    for n in range(1, 4):
        mine = mine + total[n * SHARE : (n + 1) * SHARE]
    mine = jnp.concatenate([mine * (1.0 / N)] * 8, axis=0).astype(BF16)
    for n in range(DEV // 8):
        out[8 * SHARE * n : 8 * SHARE * (n + 1)] = mine


def split_kernel(sums, grad_proj, grad_gate, grad_out):
    whole = sums[...].astype(F32)
    for part in range(4):
        grad_proj[:, part * CH : (part + 1) * CH] = whole[part * CH : (part + 1) * CH].T
    grad_gate[...] = whole[4 * CH : 5 * CH].T
    grad_out[...] = whole[5 * CH :]


def call(kernel, outs, scratch, flops, args, in_hbm=False, vmem=16):
    space = pltpu.HBM if in_hbm else pltpu.VMEM
    moved = sum(x.size * x.dtype.itemsize for x in args) + sum(
        x.size * x.dtype.itemsize for x in outs
    )
    if in_hbm:
        args = [pltpu.with_memory_space_constraint(x, pltpu.HBM) for x in args]
    return pl.pallas_call(
        kernel,
        out_shape=outs,
        in_specs=[pl.BlockSpec(memory_space=space)] * len(args),
        out_specs=[pl.BlockSpec(memory_space=pltpu.VMEM)] * len(outs),
        scratch_shapes=scratch,
        compiler_params=pltpu.CompilerParams(vmem_limit_bytes=vmem << 20),
        cost_estimate=pl.CostEstimate(flops=flops, bytes_accessed=moved, transcendentals=0),
    )(*args)


def exchange(x):
    return lax.all_to_all(x, AXES, 0, 0, tiled=True)


def exchange_terms(x):
    return exchange(x.reshape(DEV, SHARE // 2, 2, LANES)).reshape(x.shape)


def split_rows(x):
    return x.reshape(DEV, -1, LANES)


def join_rows(x):
    return x.reshape(DEV, -1)


def body(
    pair,
    cotangent,
    res_mask,
    chain,
    ln_in_gain,
    ln_in_bias,
    w_proj,
    w_gate,
    chain_bias,
    ln_out_gain,
    ln_out_bias,
    w_out,
):
    S = jax.ShapeDtypeStruct
    V = pltpu.VMEM
    unit = 2 * PAIRS * CH * CH

    def flat(x):
        return x.reshape(1, -1)

    send_ab, zn_t, grad_update, q, slope, factor = call(
        front_kernel,
        [
            S((CH, 2 * PAIRS), BF16), S((CH, PAIRS), BF16), S((CH, PAIRS), BF16),
            S((CH, PAIRS), F32), S((CH, PAIRS), F32), S((4 * CH, PAIRS), BF16),
        ],
        [
            pltpu.SMEM((N,), jnp.int32), pltpu.SMEM((N,), jnp.int32),
            V((1, CH), F32), V((1, CH), F32), V((1, CH), F32), V((1, CH), F32),
            V((CH, 4 * CH), BF16), V((CH, CH), BF16), V((CH, CH), BF16),
            V((ROWS, COLS, CH), BF16), V((ROWS, COLS, CH), BF16),
            V((ROWS, COLS, CH), F32), V((ROWS, COLS, CH), F32),
            V((4 * CH, CH), BF16), V((CH, CH), BF16),
            pltpu.SemaphoreType.DMA((9 + 2 * PIECES,)),
        ],
        6 * unit,
        (
            res_mask, chain, flat(ln_in_gain), flat(ln_in_bias), flat(chain_bias),
            flat(ln_out_gain), w_proj, w_gate, w_out, pair, cotangent,
        ),
        in_hbm=True,
    )
    recv_ab = exchange(split_rows(send_ab))
    send_mixed, a_t, b_t = call(
        mix_kernel,
        [S((DEV, CHUNKS, LANES), BF16), S((N, N), BF16), S((N, N), BF16)],
        [V((TILES, N, LANES), F32)],
        2 * N * N * N,
        (recv_ab,),
    )
    send_grad, y = call(
        middle_kernel,
        [S((CH, PAIRS), BF16), S((CH, PAIRS), BF16)],
        [],
        0,
        (join_rows(exchange(send_mixed)), q, flat(ln_out_gain), flat(ln_out_bias)),
    )
    (send_back,) = call(
        unmix_kernel,
        [S((DEV, 2 * CHUNKS, LANES), BF16)],
        [V((TILES, N, LANES), F32), V((N, N), BF16)],
        4 * N * N * N,
        (exchange(split_rows(send_grad)), a_t, b_t),
    )
    terms, grad_p, logit_t = call(
        back_kernel,
        [S((6 * CH, CH), BF16), S((4 * CH, PAIRS), BF16), S((CH, PAIRS), BF16)],
        [V((CH, CH), BF16)],
        7 * unit,
        (join_rows(exchange(send_back)), zn_t, factor, y, slope, grad_update, w_out),
    )
    parts = exchange_terms(terms)
    (summed,) = call(sum_kernel, [S((6 * CH, CH), BF16)], [], 0, (parts,))
    summed, grad_p, logit_t = lax.optimization_barrier((summed, grad_p, logit_t))
    sums = exchange_terms(summed)
    (grad_pair,) = call(
        last_kernel,
        [S((ROWS, COLS, CH), BF16)],
        [V((PAIRS, CH), F32)],
        5 * unit,
        (grad_p, logit_t, pair, flat(ln_in_gain), w_proj, w_gate),
    )
    grad_proj, grad_gate, grad_out = call(
        split_kernel, [S((CH, 4 * CH), F32), S((CH, CH), F32), S((CH, CH), F32)], [], 0, (sums,)
    )
    return (grad_pair, grad_proj, grad_gate, grad_out)


def solution(mesh):
    return jax.shard_map(
        body,
        mesh=mesh,
        in_specs=(P("row", "col", None), P("row", "col", None)) + (P(),) * 10,
        out_specs=(P("row", "col", None), P(), P(), P()),
        check_vma=False,
    )
```

```python
import functools

import jax
import jax.numpy as jnp
from jax import lax
from jax.experimental import pallas as pl
from jax.experimental.pallas import tpu as pltpu
from jax.sharding import PartitionSpec as P

EPS = 1e-05
F32 = jnp.float32
BF16 = jnp.bfloat16
AXES = ("row", "col")

ROWS = 64
COLS = 32
NROW = 8
NCOL = 16
DEV = NROW * NCOL
CH = 128
N = 512
PAIRS = ROWS * COLS
LANES = 128
CHUNKS = PAIRS // LANES
WIDE = 256
STEPS = PAIRS // WIDE
EACH = WIDE // ROWS
TILES = N // LANES
SHARE = 6 * CH // DEV


def dot(left, right, dim_left, dim_right):
    return lax.dot_general(
        left, right, (((dim_left,), (dim_right,)), ((), ())), preferred_element_type=F32
    )


def column(row):
    return jnp.broadcast_to(row, (WIDE, row.shape[1])).T


def lanes_of(s, offset=0):
    return slice(offset + s * WIDE, offset + (s + 1) * WIDE)


def swap_halves(first, second):
    low = lax.broadcasted_iota(jnp.int32, first.shape, 1) < LANES // 2
    return (
        jnp.where(low, first, pltpu.roll(second, LANES // 2, 1)),
        jnp.where(low, pltpu.roll(first, LANES // 2, 1), second),
    )


def load_chunk(ref, s):
    parts = [ref[pl.ds(EACH * s + e, ROWS, stride=COLS), :] for e in range(EACH)]
    return jnp.concatenate(parts, axis=0).astype(BF16).T.astype(F32)


def store_chunk(ref, s, value):
    value = value.astype(BF16).T.astype(F32)
    for e in range(EACH):
        ref[pl.ds(EACH * s + e, ROWS, stride=COLS), :] = value[e * ROWS : (e + 1) * ROWS]


def loop(step):
    for s in range(STEPS):
        step(s)


def fetch(sems, first, *routes):
    copies = [
        pltpu.make_async_copy(src, dst, sems.at[first + n]) for n, (src, dst) in enumerate(routes)
    ]
    for copy in copies:
        copy.start()
    return copies


LANE = (1, LANES)


def spread_rows(values, row_start):
    place = lax.broadcasted_iota(jnp.int32, LANE, 1) % ROWS
    out = jnp.zeros(LANE, jnp.int32)
    for i in range(ROWS):
        out = jnp.where(place == i, values[row_start + i], out)
    return out


def pick(values, col_start, s, combine):
    low = lax.broadcasted_iota(jnp.int32, LANE, 1) < ROWS
    parts = []
    for e in range(0, EACH, 2):
        k = col_start + EACH * s + e
        parts.append(combine(jnp.where(low, values[k], values[k + 1])).astype(F32))
    return jnp.concatenate(parts, axis=1)


def front_kernel(
    mask_h, gain_h, bias_h, w_proj_h, pair_h,
    send, zn_t, factor,
    mask_s, gain, bias, w_proj, pair, xs, wp_t, sems,
):
    copies = fetch(
        sems, 0, (mask_h, mask_s), (gain_h, gain), (bias_h, bias), (w_proj_h, w_proj), (pair_h, pair)
    )
    for copy in copies[:4]:
        copy.wait()
    row_start = lax.axis_index("row") * ROWS
    col_start = lax.axis_index("col") * COLS
    for n in range(4):
        weights = w_proj[:, n * CH : (n + 1) * CH].astype(F32).T
        wp_t[n * CH : (n + 1) * CH] = (weights if n % 2 else 0.5 * weights).astype(BF16)
    columns = jnp.concatenate([gain[...], bias[...], jnp.zeros((6, CH), F32)], axis=0).T
    gain_c, bias_c = (jnp.broadcast_to(columns[:, n : n + 1], (CH, WIDE)) for n in range(2))
    mask_row = spread_rows(mask_s, row_start)
    copies[4].wait()
    xs[...] = pair[...].astype(F32)
    for s in range(STEPS):
        here = lanes_of(s)
        x = load_chunk(xs.reshape(PAIRS, CH), s)
        mean = jnp.mean(x, axis=0, keepdims=True)
        centred = x - mean
        inverse = lax.rsqrt(jnp.mean(centred * centred, axis=0, keepdims=True) + EPS)
        zn = (centred * inverse * gain_c + bias_c).astype(BF16)
        zn_t[:, here] = zn
        half = 0.5 * pick(mask_s, col_start, s, lambda other: other * mask_row)
        proj = dot(wp_t[...], zn, 1, 0)
        for side in range(2):
            base = 2 * CH * side
            plain = jnp.tanh(proj[base : base + CH]) * half + half
            act = plain * proj[base + CH : base + 2 * CH]
            send[:, lanes_of(s, side * PAIRS)] = act.astype(BF16)
            factor[base : base + CH, here] = (act - act * plain).astype(BF16)
            factor[base + CH : base + 2 * CH, here] = plain.astype(BF16)


def mix_kernel(
    chain_h, chain_bias, out_gain, w_gate, w_out, cot, zn_t, recv,
    send, a_t, b_t, grad_update, q_out, slope,
    mixed, chain_s, cs, wg_t, sems,
):
    (copy,) = fetch(sems, 0, (chain_h, chain_s))
    cs[...] = cot[...].astype(F32)
    wg_t[...] = (0.5 * w_gate[...].astype(F32).T).astype(BF16)
    columns = jnp.concatenate(
        [0.5 * chain_bias[...], out_gain[...], jnp.zeros((6, CH), F32)], axis=0
    ).T
    chain_c, out_gain_c = (jnp.broadcast_to(columns[:, n : n + 1], (CH, WIDE)) for n in range(2))
    for c in range(NCOL):
        for t in range(TILES):
            for offset, out in ((0, a_t), (CHUNKS, b_t)):
                rows = slice(offset, offset + CHUNKS)
                first = recv[32 * t + c, rows].astype(F32)
                second = recv[32 * t + 16 + c, rows].astype(F32)
                even, odd = swap_halves(first, second)
                spot = slice(t * LANES, (t + 1) * LANES)
                out[32 * c : 32 * c + 16, spot] = even.astype(BF16)
                out[32 * c + 16 : 32 * c + 32, spot] = odd.astype(BF16)
    product = dot(b_t[...], a_t[...], 0, 0)
    for t in range(TILES):
        mixed[t] = product[:, t * LANES : (t + 1) * LANES]
    copy.wait()
    row_start = lax.axis_index("row") * ROWS
    col_start = lax.axis_index("col") * COLS
    chain_row = spread_rows(chain_s, row_start)
    for s in range(STEPS):
        here = lanes_of(s)
        same = pick(chain_s, col_start, s, lambda other: other == chain_row)
        gate = 0.5 * jnp.tanh(dot(wg_t[...], zn_t[:, here], 1, 0) + same * chain_c) + 0.5
        gated = load_chunk(cs.reshape(PAIRS, CH), s) * gate
        update = gated.astype(BF16)
        grad_update[:, here] = update
        slope[:, here] = gated - gated * gate
        q_out[:, here] = dot(w_out[...], update, 1, 0) * out_gain_c
    for c in range(NCOL):
        for t in range(TILES):
            first = mixed[t, pl.ds(32 * c, CHUNKS, stride=2), :]
            second = mixed[t, pl.ds(32 * c + 1, CHUNKS, stride=2), :]
            even, odd = swap_halves(first, second)
            send[32 * t + c] = even.astype(BF16)
            send[32 * t + 16 + c] = odd.astype(BF16)


def middle_kernel(recv, q_in, gain, bias, send, y_out):
    gain_c = column(gain[...])
    bias_c = column(bias[...])

    def step(s):
        here = lanes_of(s)
        mixed = recv[:, here].astype(F32)
        mean = jnp.mean(mixed, axis=0, keepdims=True)
        centred = mixed - mean
        inverse = lax.rsqrt(jnp.mean(centred * centred, axis=0, keepdims=True) + EPS)
        normed = centred * inverse
        y_out[:, here] = (normed * gain_c + bias_c).astype(BF16)
        q = q_in[:, here]
        first = jnp.mean(q, axis=0, keepdims=True)
        second = jnp.mean(q * normed, axis=0, keepdims=True)
        send[:, here] = ((q - first - normed * second) * inverse).astype(BF16)

    loop(step)


def unmix_kernel(recv, a_t, b_t, send, strided, grad):
    for c in range(NCOL):
        for t in range(TILES):
            even, odd = swap_halves(
                recv[32 * t + c].astype(F32), recv[32 * t + 16 + c].astype(F32)
            )
            strided[t, pl.ds(32 * c, CHUNKS, stride=2), :] = even
            strided[t, pl.ds(32 * c + 1, CHUNKS, stride=2), :] = odd
    for t in range(TILES):
        grad[:, t * LANES : (t + 1) * LANES] = strided[t].astype(BF16)
    for offset, left, dim in ((0, b_t, 0), (CHUNKS, a_t, 1)):
        product = dot(left[...], grad[...], 1, dim)
        rows = slice(offset, offset + CHUNKS)
        for c in range(NCOL):
            for t in range(TILES):
                spot = slice(t * LANES, (t + 1) * LANES)
                even, odd = swap_halves(
                    product[32 * c : 32 * c + 16, spot], product[32 * c + 16 : 32 * c + 32, spot]
                )
                send[32 * t + c, rows] = even.astype(BF16)
                send[32 * t + 16 + c, rows] = odd.astype(BF16)


def back_kernel(
    recv, zn_t, factor, y, slope, grad_update, w_out, terms, grad_p, logit_t, wo_t
):
    wo_t[...] = w_out[...].astype(F32).T.astype(BF16)

    def step(s):
        here = lanes_of(s)
        update = dot(wo_t[...], y[:, here], 1, 0)
        logit_t[:, here] = (slope[:, here] * update).astype(BF16)
        for part in range(4):
            rows = slice(part * CH, (part + 1) * CH)
            grad_p[rows, here] = recv[:, lanes_of(s, (part // 2) * PAIRS)] * factor[rows, here]

    loop(step)
    zn = zn_t[...].T
    terms[: 4 * CH] = dot(grad_p[...], zn, 1, 0).astype(BF16)
    terms[4 * CH : 5 * CH] = dot(logit_t[...], zn, 1, 0).astype(BF16)
    terms[5 * CH :] = dot(y[...], grad_update[...], 1, 1).astype(BF16)


def last_kernel(grad_p, logit_t, pair, gain, w_proj, w_gate, grad_pair, xs):
    gain_c = column(gain[...])
    xs[...] = pair[...].astype(F32).reshape(PAIRS, CH)

    def step(s):
        here = lanes_of(s)
        grad_zn = dot(w_proj[...], grad_p[:, here], 1, 0) + dot(w_gate[...], logit_t[:, here], 1, 0)
        x = load_chunk(xs, s)
        centred = x - jnp.mean(x, axis=0, keepdims=True)
        inverse = lax.rsqrt(jnp.mean(centred * centred, axis=0, keepdims=True) + EPS)
        normed = centred * inverse
        q = grad_zn * gain_c
        first = jnp.mean(q, axis=0, keepdims=True)
        second = jnp.mean(q * normed, axis=0, keepdims=True)
        store_chunk(xs, s, (q - first - normed * second) * inverse)

    loop(step)
    grad_pair[...] = xs[...].reshape(ROWS, COLS, CH).astype(BF16)


def sum_kernel(parts, out):
    total = parts[...].astype(F32).reshape(DEV // 4, 4 * SHARE, LANES)
    while total.shape[0] > 1:
        half = total.shape[0] // 2
        total = total[:half] + total[half:]
    total = total[0]
    mine = total[:SHARE]
    for n in range(1, 4):
        mine = mine + total[n * SHARE : (n + 1) * SHARE]
    mine = jnp.concatenate([mine * (1.0 / N)] * 8, axis=0).astype(BF16)
    for n in range(DEV // 8):
        out[8 * SHARE * n : 8 * SHARE * (n + 1)] = mine


def split_kernel(sums, grad_proj, grad_gate, grad_out):
    whole = sums[...].astype(F32)
    for part in range(4):
        grad_proj[:, part * CH : (part + 1) * CH] = whole[part * CH : (part + 1) * CH].T
    grad_gate[...] = whole[4 * CH : 5 * CH].T
    grad_out[...] = whole[5 * CH :]


def call(kernel, outs, scratch, flops, args, hbm=0, vmem=16):
    moved = sum(x.size * x.dtype.itemsize for x in args) + sum(
        x.size * x.dtype.itemsize for x in outs
    )
    spaces = [pltpu.HBM] * hbm + [pltpu.VMEM] * (len(args) - hbm)
    args = [
        pltpu.with_memory_space_constraint(x, pltpu.HBM) if n < hbm else x
        for n, x in enumerate(args)
    ]
    return pl.pallas_call(
        kernel,
        out_shape=outs,
        in_specs=[pl.BlockSpec(memory_space=space) for space in spaces],
        out_specs=[pl.BlockSpec(memory_space=pltpu.VMEM)] * len(outs),
        scratch_shapes=scratch,
        compiler_params=pltpu.CompilerParams(vmem_limit_bytes=vmem << 20),
        cost_estimate=pl.CostEstimate(flops=flops, bytes_accessed=moved, transcendentals=0),
    )(*args)


def exchange(x):
    return lax.all_to_all(x, AXES, 0, 0, tiled=True)


def exchange_terms(x):
    split = x.reshape(DEV, SHARE // 2, 2, LANES)
    return lax.all_to_all(split, AXES[::-1], 0, 0, tiled=True).reshape(x.shape)


def split_rows(x):
    return x.reshape(DEV, -1, LANES)


def join_rows(x):
    return x.reshape(DEV, -1)


def body(
    pair,
    cotangent,
    res_mask,
    chain,
    ln_in_gain,
    ln_in_bias,
    w_proj,
    w_gate,
    chain_bias,
    ln_out_gain,
    ln_out_bias,
    w_out,
):
    S = jax.ShapeDtypeStruct
    V = pltpu.VMEM
    unit = 2 * PAIRS * CH * CH

    def flat(x):
        return x.reshape(1, -1)

    send_ab, zn_t, factor = call(
        front_kernel,
        [S((CH, 2 * PAIRS), BF16), S((CH, PAIRS), BF16), S((4 * CH, PAIRS), BF16)],
        [
            pltpu.SMEM((N,), jnp.int32), V((1, CH), F32), V((1, CH), F32), V((CH, 4 * CH), BF16),
            V((ROWS, COLS, CH), BF16), V((ROWS, COLS, CH), F32), V((4 * CH, CH), BF16),
            pltpu.SemaphoreType.DMA((5,)),
        ],
        4 * unit,
        (res_mask, flat(ln_in_gain), flat(ln_in_bias), w_proj, pair),
        hbm=5,
    )
    recv_ab = exchange(split_rows(send_ab))
    send_mixed, a_t, b_t, grad_update, q, slope = call(
        mix_kernel,
        [
            S((DEV, CHUNKS, LANES), BF16), S((N, N), BF16), S((N, N), BF16),
            S((CH, PAIRS), BF16), S((CH, PAIRS), F32), S((CH, PAIRS), F32),
        ],
        [
            V((TILES, N, LANES), F32), pltpu.SMEM((N,), jnp.int32), V((ROWS, COLS, CH), F32),
            V((CH, CH), BF16), pltpu.SemaphoreType.DMA((1,)),
        ],
        2 * N * N * N + 2 * unit,
        (
            chain, flat(chain_bias), flat(ln_out_gain), w_gate, w_out, cotangent, zn_t, recv_ab,
        ),
        hbm=1,
    )
    send_grad, y = call(
        middle_kernel,
        [S((CH, PAIRS), BF16), S((CH, PAIRS), BF16)],
        [],
        0,
        (join_rows(exchange(send_mixed)), q, flat(ln_out_gain), flat(ln_out_bias)),
    )
    (send_back,) = call(
        unmix_kernel,
        [S((DEV, 2 * CHUNKS, LANES), BF16)],
        [V((TILES, N, LANES), F32), V((N, N), BF16)],
        4 * N * N * N,
        (exchange(split_rows(send_grad)), a_t, b_t),
    )
    terms, grad_p, logit_t = call(
        back_kernel,
        [S((6 * CH, CH), BF16), S((4 * CH, PAIRS), BF16), S((CH, PAIRS), BF16)],
        [V((CH, CH), BF16)],
        7 * unit,
        (join_rows(exchange(send_back)), zn_t, factor, y, slope, grad_update, w_out),
    )
    parts = exchange_terms(terms)
    (summed,) = call(sum_kernel, [S((6 * CH, CH), BF16)], [], 0, (parts,))
    summed, grad_p, logit_t = lax.optimization_barrier((summed, grad_p, logit_t))
    sums = exchange_terms(summed)
    (grad_pair,) = call(
        last_kernel,
        [S((ROWS, COLS, CH), BF16)],
        [V((PAIRS, CH), F32)],
        5 * unit,
        (grad_p, logit_t, pair, flat(ln_in_gain), w_proj, w_gate),
    )
    grad_proj, grad_gate, grad_out = call(
        split_kernel, [S((CH, 4 * CH), F32), S((CH, CH), F32), S((CH, CH), F32)], [], 0, (sums,)
    )
    return (grad_pair, grad_proj, grad_gate, grad_out)


def solution(mesh):
    return jax.shard_map(
        body,
        mesh=mesh,
        in_specs=(P("row", "col", None), P("row", "col", None)) + (P(),) * 10,
        out_specs=(P("row", "col", None), P(), P(), P()),
        check_vma=False,
    )
```

```python
import functools

import jax
import jax.numpy as jnp
from jax import lax
from jax.experimental import pallas as pl
from jax.experimental.pallas import tpu as pltpu
from jax.sharding import PartitionSpec as P

EPS = 1e-05
F32 = jnp.float32
BF16 = jnp.bfloat16
AXES = ("row", "col")

ROWS = 64
COLS = 32
NROW = 8
NCOL = 16
DEV = NROW * NCOL
CH = 128
N = 512
PAIRS = ROWS * COLS
LANES = 128
CHUNKS = PAIRS // LANES
WIDE = 256
STEPS = PAIRS // WIDE
EACH = WIDE // ROWS
TILES = N // LANES
SHARE = 6 * CH // DEV


def dot(left, right, dim_left, dim_right):
    return lax.dot_general(
        left, right, (((dim_left,), (dim_right,)), ((), ())), preferred_element_type=F32
    )


def column(row):
    return jnp.broadcast_to(row, (WIDE, row.shape[1])).T


def lanes_of(s, offset=0):
    return slice(offset + s * WIDE, offset + (s + 1) * WIDE)


def swap_halves(first, second):
    low = lax.broadcasted_iota(jnp.int32, first.shape, 1) < LANES // 2
    return (
        jnp.where(low, first, pltpu.roll(second, LANES // 2, 1)),
        jnp.where(low, pltpu.roll(first, LANES // 2, 1), second),
    )


def load_chunk(ref, s):
    parts = [ref[pl.ds(EACH * s + e, ROWS, stride=COLS), :] for e in range(EACH)]
    return jnp.concatenate(parts, axis=0).astype(BF16).T.astype(F32)


def store_chunk(ref, s, value):
    value = value.astype(BF16).T.astype(F32)
    for e in range(EACH):
        ref[pl.ds(EACH * s + e, ROWS, stride=COLS), :] = value[e * ROWS : (e + 1) * ROWS]


def loop(step):
    for s in range(STEPS):
        step(s)


def fetch(sems, first, *routes):
    copies = [
        pltpu.make_async_copy(src, dst, sems.at[first + n]) for n, (src, dst) in enumerate(routes)
    ]
    for copy in copies:
        copy.start()
    return copies


LANE = (1, LANES)


def spread_rows(values, row_start):
    place = lax.broadcasted_iota(jnp.int32, LANE, 1) % ROWS
    out = jnp.zeros(LANE, jnp.int32)
    for i in range(ROWS):
        out = jnp.where(place == i, values[row_start + i], out)
    return out


def pick(values, col_start, s, combine):
    low = lax.broadcasted_iota(jnp.int32, LANE, 1) < ROWS
    parts = []
    for e in range(0, EACH, 2):
        k = col_start + EACH * s + e
        parts.append(combine(jnp.where(low, values[k], values[k + 1])).astype(F32))
    return jnp.concatenate(parts, axis=1)


def front_kernel(
    mask_h, gain_h, bias_h, w_proj_h, pair_h,
    send, zn_t, factor,
    mask_s, gain, bias, w_proj, pair, xs, wp_t, sems,
):
    copies = fetch(
        sems, 0, (mask_h, mask_s), (gain_h, gain), (bias_h, bias), (w_proj_h, w_proj), (pair_h, pair)
    )
    for copy in copies[:4]:
        copy.wait()
    row_start = lax.axis_index("row") * ROWS
    col_start = lax.axis_index("col") * COLS
    for n in range(4):
        weights = w_proj[:, n * CH : (n + 1) * CH].astype(F32).T
        wp_t[n * CH : (n + 1) * CH] = (weights if n % 2 else 0.5 * weights).astype(BF16)
    columns = jnp.concatenate([gain[...], bias[...], jnp.zeros((6, CH), F32)], axis=0).T
    gain_c, bias_c = (jnp.broadcast_to(columns[:, n : n + 1], (CH, WIDE)) for n in range(2))
    mask_row = spread_rows(mask_s, row_start)
    copies[4].wait()
    xs[...] = pair[...].astype(F32)
    for s in range(STEPS):
        here = lanes_of(s)
        x = load_chunk(xs.reshape(PAIRS, CH), s)
        mean = jnp.mean(x, axis=0, keepdims=True)
        centred = x - mean
        inverse = lax.rsqrt(jnp.mean(centred * centred, axis=0, keepdims=True) + EPS)
        zn = (centred * inverse * gain_c + bias_c).astype(BF16)
        zn_t[:, here] = zn
        half = 0.5 * pick(mask_s, col_start, s, lambda other: other * mask_row)
        proj = dot(wp_t[...], zn, 1, 0)
        for side in range(2):
            base = 2 * CH * side
            plain = jnp.tanh(proj[base : base + CH]) * half + half
            act = plain * proj[base + CH : base + 2 * CH]
            send[:, lanes_of(s, side * PAIRS)] = act.astype(BF16)
            factor[base : base + CH, here] = (act - act * plain).astype(BF16)
            factor[base + CH : base + 2 * CH, here] = plain.astype(BF16)


def mix_kernel(
    chain_h, chain_bias, out_gain, w_gate, w_out, cot, zn_t, recv,
    send, a_t, b_t, grad_update, q_out, slope,
    mixed, chain_s, cs, wg_t, sems,
):
    (copy,) = fetch(sems, 0, (chain_h, chain_s))
    cs[...] = cot[...].astype(F32)
    wg_t[...] = (0.5 * w_gate[...].astype(F32).T).astype(BF16)
    columns = jnp.concatenate(
        [0.5 * chain_bias[...], out_gain[...], jnp.zeros((6, CH), F32)], axis=0
    ).T
    chain_c, out_gain_c = (jnp.broadcast_to(columns[:, n : n + 1], (CH, WIDE)) for n in range(2))
    for c in range(NCOL):
        for t in range(TILES):
            for offset, out in ((0, a_t), (CHUNKS, b_t)):
                rows = slice(offset, offset + CHUNKS)
                first = recv[32 * t + c, rows].astype(F32)
                second = recv[32 * t + 16 + c, rows].astype(F32)
                even, odd = swap_halves(first, second)
                spot = slice(t * LANES, (t + 1) * LANES)
                out[32 * c : 32 * c + 16, spot] = even.astype(BF16)
                out[32 * c + 16 : 32 * c + 32, spot] = odd.astype(BF16)
    product = dot(b_t[...], a_t[...], 0, 0)
    for t in range(TILES):
        mixed[t] = product[:, t * LANES : (t + 1) * LANES]
    copy.wait()
    row_start = lax.axis_index("row") * ROWS
    col_start = lax.axis_index("col") * COLS
    chain_row = spread_rows(chain_s, row_start)
    for s in range(STEPS):
        here = lanes_of(s)
        same = pick(chain_s, col_start, s, lambda other: other == chain_row)
        gate = 0.5 * jnp.tanh(dot(wg_t[...], zn_t[:, here], 1, 0) + same * chain_c) + 0.5
        gated = load_chunk(cs.reshape(PAIRS, CH), s) * gate
        update = gated.astype(BF16)
        grad_update[:, here] = update
        slope[:, here] = gated - gated * gate
        q_out[:, here] = dot(w_out[...], update, 1, 0) * out_gain_c
    for c in range(NCOL):
        for t in range(TILES):
            first = mixed[t, pl.ds(32 * c, CHUNKS, stride=2), :]
            second = mixed[t, pl.ds(32 * c + 1, CHUNKS, stride=2), :]
            even, odd = swap_halves(first, second)
            send[32 * t + c] = even.astype(BF16)
            send[32 * t + 16 + c] = odd.astype(BF16)


def middle_kernel(recv, q_in, gain, bias, send, y_out):
    gain_c = column(gain[...])
    bias_c = column(bias[...])

    def step(s):
        here = lanes_of(s)
        mixed = recv[:, here].astype(F32)
        mean = jnp.mean(mixed, axis=0, keepdims=True)
        centred = mixed - mean
        inverse = lax.rsqrt(jnp.mean(centred * centred, axis=0, keepdims=True) + EPS)
        normed = centred * inverse
        y_out[:, here] = (normed * gain_c + bias_c).astype(BF16)
        q = q_in[:, here]
        first = jnp.mean(q, axis=0, keepdims=True)
        second = jnp.mean(q * normed, axis=0, keepdims=True)
        send[:, here] = ((q - first - normed * second) * inverse).astype(BF16)

    loop(step)


def unmix_kernel(recv, a_t, b_t, send, strided, grad):
    for c in range(NCOL):
        for t in range(TILES):
            even, odd = swap_halves(
                recv[32 * t + c].astype(F32), recv[32 * t + 16 + c].astype(F32)
            )
            strided[t, pl.ds(32 * c, CHUNKS, stride=2), :] = even
            strided[t, pl.ds(32 * c + 1, CHUNKS, stride=2), :] = odd
    for t in range(TILES):
        grad[:, t * LANES : (t + 1) * LANES] = strided[t].astype(BF16)
    for offset, left, dim in ((0, b_t, 0), (CHUNKS, a_t, 1)):
        product = dot(left[...], grad[...], 1, dim)
        rows = slice(offset, offset + CHUNKS)
        for c in range(NCOL):
            for t in range(TILES):
                spot = slice(t * LANES, (t + 1) * LANES)
                even, odd = swap_halves(
                    product[32 * c : 32 * c + 16, spot], product[32 * c + 16 : 32 * c + 32, spot]
                )
                send[32 * t + c, rows] = even.astype(BF16)
                send[32 * t + 16 + c, rows] = odd.astype(BF16)


def back_kernel(
    recv, zn_t, factor, y, slope, grad_update, w_out, terms, grad_p, logit_t, wo_t
):
    wo_t[...] = w_out[...].astype(F32).T.astype(BF16)

    def step(s):
        here = lanes_of(s)
        update = dot(wo_t[...], y[:, here], 1, 0)
        logit_t[:, here] = (slope[:, here] * update).astype(BF16)
        for part in range(4):
            rows = slice(part * CH, (part + 1) * CH)
            grad_p[rows, here] = recv[:, lanes_of(s, (part // 2) * PAIRS)] * factor[rows, here]

    loop(step)
    zn = zn_t[...].T
    terms[: 4 * CH] = dot(grad_p[...], zn, 1, 0).astype(BF16)
    terms[4 * CH : 5 * CH] = dot(logit_t[...], zn, 1, 0).astype(BF16)
    terms[5 * CH :] = dot(y[...], grad_update[...], 1, 1).astype(BF16)


def last_kernel(grad_p, logit_t, pair, gain, w_proj, w_gate, grad_pair, xs):
    gain_c = column(gain[...])
    xs[...] = pair[...].astype(F32).reshape(PAIRS, CH)

    def step(s):
        here = lanes_of(s)
        grad_zn = dot(w_proj[...], grad_p[:, here], 1, 0) + dot(w_gate[...], logit_t[:, here], 1, 0)
        x = load_chunk(xs, s)
        centred = x - jnp.mean(x, axis=0, keepdims=True)
        inverse = lax.rsqrt(jnp.mean(centred * centred, axis=0, keepdims=True) + EPS)
        normed = centred * inverse
        q = grad_zn * gain_c
        first = jnp.mean(q, axis=0, keepdims=True)
        second = jnp.mean(q * normed, axis=0, keepdims=True)
        store_chunk(xs, s, (q - first - normed * second) * inverse)

    loop(step)
    grad_pair[...] = xs[...].reshape(ROWS, COLS, CH).astype(BF16)


def sum_kernel(parts, out):
    total = parts[...].astype(F32).reshape(DEV // 4, 4 * SHARE, LANES)
    while total.shape[0] > 1:
        half = total.shape[0] // 2
        total = total[:half] + total[half:]
    total = total[0]
    mine = total[:SHARE]
    for n in range(1, 4):
        mine = mine + total[n * SHARE : (n + 1) * SHARE]
    mine = jnp.concatenate([mine * (1.0 / N)] * 8, axis=0).astype(BF16)
    for n in range(DEV // 8):
        out[8 * SHARE * n : 8 * SHARE * (n + 1)] = mine


def split_kernel(sums, grad_proj, grad_gate, grad_out, wide, gate, out, sems):
    copies = []
    for part in range(4):
        spot = slice(part * CH, (part + 1) * CH)
        wide[:, spot] = sums[spot].astype(F32).T
        copies += fetch(sems, part, (wide.at[:, spot], grad_proj.at[:, spot]))
    gate[...] = sums[4 * CH : 5 * CH].astype(F32).T
    copies += fetch(sems, 4, (gate, grad_gate))
    out[...] = sums[5 * CH :].astype(F32)
    copies += fetch(sems, 5, (out, grad_out))
    for copy in copies:
        copy.wait()


def call(kernel, outs, scratch, flops, args, hbm=0, out_space=pltpu.VMEM, vmem=16):
    moved = sum(x.size * x.dtype.itemsize for x in args) + sum(
        x.size * x.dtype.itemsize for x in outs
    )
    spaces = [pltpu.HBM] * hbm + [pltpu.VMEM] * (len(args) - hbm)
    args = [
        pltpu.with_memory_space_constraint(x, pltpu.HBM) if n < hbm else x
        for n, x in enumerate(args)
    ]
    return pl.pallas_call(
        kernel,
        out_shape=outs,
        in_specs=[pl.BlockSpec(memory_space=space) for space in spaces],
        out_specs=[pl.BlockSpec(memory_space=out_space)] * len(outs),
        scratch_shapes=scratch,
        compiler_params=pltpu.CompilerParams(vmem_limit_bytes=vmem << 20),
        cost_estimate=pl.CostEstimate(flops=flops, bytes_accessed=moved, transcendentals=0),
    )(*args)


def exchange(x):
    return lax.all_to_all(x, AXES, 0, 0, tiled=True)


def exchange_terms(x):
    split = x.reshape(DEV, SHARE // 2, 2, LANES)
    return lax.all_to_all(split, AXES[::-1], 0, 0, tiled=True).reshape(x.shape)


def split_rows(x):
    return x.reshape(DEV, -1, LANES)


def join_rows(x):
    return x.reshape(DEV, -1)


def body(
    pair,
    cotangent,
    res_mask,
    chain,
    ln_in_gain,
    ln_in_bias,
    w_proj,
    w_gate,
    chain_bias,
    ln_out_gain,
    ln_out_bias,
    w_out,
):
    S = jax.ShapeDtypeStruct
    V = pltpu.VMEM
    unit = 2 * PAIRS * CH * CH

    def flat(x):
        return x.reshape(1, -1)

    send_ab, zn_t, factor = call(
        front_kernel,
        [S((CH, 2 * PAIRS), BF16), S((CH, PAIRS), BF16), S((4 * CH, PAIRS), BF16)],
        [
            pltpu.SMEM((N,), jnp.int32), V((1, CH), F32), V((1, CH), F32), V((CH, 4 * CH), BF16),
            V((ROWS, COLS, CH), BF16), V((ROWS, COLS, CH), F32), V((4 * CH, CH), BF16),
            pltpu.SemaphoreType.DMA((5,)),
        ],
        4 * unit,
        (res_mask, flat(ln_in_gain), flat(ln_in_bias), w_proj, pair),
        hbm=5,
    )
    recv_ab = exchange(split_rows(send_ab))
    send_mixed, a_t, b_t, grad_update, q, slope = call(
        mix_kernel,
        [
            S((DEV, CHUNKS, LANES), BF16), S((N, N), BF16), S((N, N), BF16),
            S((CH, PAIRS), BF16), S((CH, PAIRS), F32), S((CH, PAIRS), F32),
        ],
        [
            V((TILES, N, LANES), F32), pltpu.SMEM((N,), jnp.int32), V((ROWS, COLS, CH), F32),
            V((CH, CH), BF16), pltpu.SemaphoreType.DMA((1,)),
        ],
        2 * N * N * N + 2 * unit,
        (
            chain, flat(chain_bias), flat(ln_out_gain), w_gate, w_out, cotangent, zn_t, recv_ab,
        ),
        hbm=1,
    )
    send_grad, y = call(
        middle_kernel,
        [S((CH, PAIRS), BF16), S((CH, PAIRS), BF16)],
        [],
        0,
        (join_rows(exchange(send_mixed)), q, flat(ln_out_gain), flat(ln_out_bias)),
    )
    (send_back,) = call(
        unmix_kernel,
        [S((DEV, 2 * CHUNKS, LANES), BF16)],
        [V((TILES, N, LANES), F32), V((N, N), BF16)],
        4 * N * N * N,
        (exchange(split_rows(send_grad)), a_t, b_t),
    )
    terms, grad_p, logit_t = call(
        back_kernel,
        [S((6 * CH, CH), BF16), S((4 * CH, PAIRS), BF16), S((CH, PAIRS), BF16)],
        [V((CH, CH), BF16)],
        7 * unit,
        (join_rows(exchange(send_back)), zn_t, factor, y, slope, grad_update, w_out),
    )
    parts = exchange_terms(terms)
    (summed,) = call(sum_kernel, [S((6 * CH, CH), BF16)], [], 0, (parts,))
    summed, grad_p, logit_t = lax.optimization_barrier((summed, grad_p, logit_t))
    sums = exchange_terms(summed)
    (grad_pair,) = call(
        last_kernel,
        [S((ROWS, COLS, CH), BF16)],
        [V((PAIRS, CH), F32)],
        5 * unit,
        (grad_p, logit_t, pair, flat(ln_in_gain), w_proj, w_gate),
    )
    grad_proj, grad_gate, grad_out = call(
        split_kernel,
        [S((CH, 4 * CH), F32), S((CH, CH), F32), S((CH, CH), F32)],
        [V((CH, 4 * CH), F32), V((CH, CH), F32), V((CH, CH), F32), pltpu.SemaphoreType.DMA((6,))],
        0,
        (sums,),
        out_space=pltpu.HBM,
    )
    return (grad_pair, grad_proj, grad_gate, grad_out)


def solution(mesh):
    return jax.shard_map(
        body,
        mesh=mesh,
        in_specs=(P("row", "col", None), P("row", "col", None)) + (P(),) * 10,
        out_specs=(P("row", "col", None), P(), P(), P()),
        check_vma=False,
    )
```

```python
import functools

import jax
import jax.numpy as jnp
from jax import lax
from jax.experimental import pallas as pl
from jax.experimental.pallas import tpu as pltpu
from jax.sharding import PartitionSpec as P

EPS = 1e-05
F32 = jnp.float32
BF16 = jnp.bfloat16
AXES = ("row", "col")

ROWS = 64
COLS = 32
NROW = 8
NCOL = 16
DEV = NROW * NCOL
CH = 128
N = 512
PAIRS = ROWS * COLS
LANES = 128
CHUNKS = PAIRS // LANES
WIDE = 256
STEPS = PAIRS // WIDE
EACH = WIDE // ROWS
TILES = N // LANES
SHARE = 6 * CH // DEV


def dot(left, right, dim_left, dim_right):
    return lax.dot_general(
        left, right, (((dim_left,), (dim_right,)), ((), ())), preferred_element_type=F32
    )


def column(row):
    return jnp.broadcast_to(row, (WIDE, row.shape[1])).T


def lanes_of(s, offset=0):
    return slice(offset + s * WIDE, offset + (s + 1) * WIDE)


def swap_halves(first, second):
    low = lax.broadcasted_iota(jnp.int32, first.shape, 1) < LANES // 2
    return (
        jnp.where(low, first, pltpu.roll(second, LANES // 2, 1)),
        jnp.where(low, pltpu.roll(first, LANES // 2, 1), second),
    )


def load_chunk(ref, s):
    parts = [ref[pl.ds(EACH * s + e, ROWS, stride=COLS), :] for e in range(EACH)]
    return jnp.concatenate(parts, axis=0).astype(BF16).T.astype(F32)


def store_chunk(ref, s, value):
    value = value.astype(BF16).T.astype(F32)
    for e in range(EACH):
        ref[pl.ds(EACH * s + e, ROWS, stride=COLS), :] = value[e * ROWS : (e + 1) * ROWS]


def loop(step):
    for s in range(STEPS):
        step(s)


def fetch(sems, first, *routes):
    copies = [
        pltpu.make_async_copy(src, dst, sems.at[first + n]) for n, (src, dst) in enumerate(routes)
    ]
    for copy in copies:
        copy.start()
    return copies


LANE = (1, LANES)


def spread_rows(values, row_start):
    place = lax.broadcasted_iota(jnp.int32, LANE, 1) % ROWS
    out = jnp.zeros(LANE, jnp.int32)
    for i in range(ROWS):
        out = jnp.where(place == i, values[row_start + i], out)
    return out


def pick(values, col_start, s, combine):
    low = lax.broadcasted_iota(jnp.int32, LANE, 1) < ROWS
    parts = []
    for e in range(0, EACH, 2):
        k = col_start + EACH * s + e
        parts.append(combine(jnp.where(low, values[k], values[k + 1])).astype(F32))
    return jnp.concatenate(parts, axis=1)


def front_kernel(
    mask_h, gain_h, bias_h, w_proj_h, pair_h,
    send, zn_t, factor,
    mask_s, gain, bias, w_proj, pair, xs, wp_t, sems,
):
    copies = fetch(
        sems, 0, (mask_h, mask_s), (gain_h, gain), (bias_h, bias), (w_proj_h, w_proj), (pair_h, pair)
    )
    for copy in copies[:4]:
        copy.wait()
    row_start = lax.axis_index("row") * ROWS
    col_start = lax.axis_index("col") * COLS
    for n in range(4):
        weights = w_proj[:, n * CH : (n + 1) * CH].astype(F32).T
        wp_t[n * CH : (n + 1) * CH] = (weights if n % 2 else 0.5 * weights).astype(BF16)
    columns = jnp.concatenate([gain[...], bias[...], jnp.zeros((6, CH), F32)], axis=0).T
    gain_c, bias_c = (jnp.broadcast_to(columns[:, n : n + 1], (CH, WIDE)) for n in range(2))
    mask_row = spread_rows(mask_s, row_start)
    copies[4].wait()
    xs[...] = pair[...].astype(F32)
    for s in range(STEPS):
        here = lanes_of(s)
        x = load_chunk(xs.reshape(PAIRS, CH), s)
        mean = jnp.mean(x, axis=0, keepdims=True)
        centred = x - mean
        inverse = lax.rsqrt(jnp.mean(centred * centred, axis=0, keepdims=True) + EPS)
        zn = (centred * inverse * gain_c + bias_c).astype(BF16)
        zn_t[:, here] = zn
        half = 0.5 * pick(mask_s, col_start, s, lambda other: other * mask_row)
        proj = dot(wp_t[...], zn, 1, 0)
        for side in range(2):
            base = 2 * CH * side
            plain = jnp.tanh(proj[base : base + CH]) * half + half
            act = plain * proj[base + CH : base + 2 * CH]
            send[:, lanes_of(s, side * PAIRS)] = act.astype(BF16)
            factor[base : base + CH, here] = (act - act * plain).astype(BF16)
            factor[base + CH : base + 2 * CH, here] = plain.astype(BF16)


def mix_kernel(
    chain_h, chain_bias, out_gain, w_gate, w_out, cot, zn_t, recv,
    send, a_t, b_t, grad_update, q_out, slope,
    mixed, chain_s, cs, wg_t, sems,
):
    (copy,) = fetch(sems, 0, (chain_h, chain_s))
    cs[...] = cot[...].astype(F32)
    wg_t[...] = (0.5 * w_gate[...].astype(F32).T).astype(BF16)
    columns = jnp.concatenate(
        [0.5 * chain_bias[...], out_gain[...], jnp.zeros((6, CH), F32)], axis=0
    ).T
    chain_c, out_gain_c = (jnp.broadcast_to(columns[:, n : n + 1], (CH, WIDE)) for n in range(2))
    for c in range(NCOL):
        for t in range(TILES):
            for offset, out in ((0, a_t), (CHUNKS, b_t)):
                rows = slice(offset, offset + CHUNKS)
                first = recv[32 * t + c, rows].astype(F32)
                second = recv[32 * t + 16 + c, rows].astype(F32)
                even, odd = swap_halves(first, second)
                spot = slice(t * LANES, (t + 1) * LANES)
                out[32 * c : 32 * c + 16, spot] = even.astype(BF16)
                out[32 * c + 16 : 32 * c + 32, spot] = odd.astype(BF16)
    product = dot(b_t[...], a_t[...], 0, 0)
    for t in range(TILES):
        mixed[t] = product[:, t * LANES : (t + 1) * LANES]
    copy.wait()
    row_start = lax.axis_index("row") * ROWS
    col_start = lax.axis_index("col") * COLS
    chain_row = spread_rows(chain_s, row_start)
    for s in range(STEPS):
        here = lanes_of(s)
        same = pick(chain_s, col_start, s, lambda other: other == chain_row)
        gate = 0.5 * jnp.tanh(dot(wg_t[...], zn_t[:, here], 1, 0) + same * chain_c) + 0.5
        gated = load_chunk(cs.reshape(PAIRS, CH), s) * gate
        update = gated.astype(BF16)
        grad_update[:, here] = update
        slope[:, here] = gated - gated * gate
        q_out[:, here] = dot(w_out[...], update, 1, 0) * out_gain_c
    for c in range(NCOL):
        for t in range(TILES):
            first = mixed[t, pl.ds(32 * c, CHUNKS, stride=2), :]
            second = mixed[t, pl.ds(32 * c + 1, CHUNKS, stride=2), :]
            even, odd = swap_halves(first, second)
            send[32 * t + c] = even.astype(BF16)
            send[32 * t + 16 + c] = odd.astype(BF16)


def middle_kernel(recv, q_in, gain, bias, send, y_out):
    gain_c = column(gain[...])
    bias_c = column(bias[...])

    def step(s):
        here = lanes_of(s)
        mixed = recv[:, here].astype(F32)
        mean = jnp.mean(mixed, axis=0, keepdims=True)
        centred = mixed - mean
        inverse = lax.rsqrt(jnp.mean(centred * centred, axis=0, keepdims=True) + EPS)
        normed = centred * inverse
        y_out[:, here] = (normed * gain_c + bias_c).astype(BF16)
        q = q_in[:, here]
        first = jnp.mean(q, axis=0, keepdims=True)
        second = jnp.mean(q * normed, axis=0, keepdims=True)
        send[:, here] = ((q - first - normed * second) * inverse).astype(BF16)

    loop(step)


def unmix_kernel(
    recv, a_t, b_t, zn_t, y, slope, grad_update, w_out, send, logit_t, terms, strided, grad, wo_t
):
    wo_t[...] = w_out[...].astype(F32).T.astype(BF16)
    for c in range(NCOL):
        for t in range(TILES):
            even, odd = swap_halves(
                recv[32 * t + c].astype(F32), recv[32 * t + 16 + c].astype(F32)
            )
            strided[t, pl.ds(32 * c, CHUNKS, stride=2), :] = even
            strided[t, pl.ds(32 * c + 1, CHUNKS, stride=2), :] = odd
    for t in range(TILES):
        grad[:, t * LANES : (t + 1) * LANES] = strided[t].astype(BF16)
    for s in range(STEPS):
        here = lanes_of(s)
        update = dot(wo_t[...], y[:, here], 1, 0)
        logit_t[:, here] = (slope[:, here] * update).astype(BF16)
    terms[:CH] = dot(logit_t[...], zn_t[...].T, 1, 0).astype(BF16)
    terms[CH:] = dot(y[...], grad_update[...], 1, 1).astype(BF16)
    for offset, left, dim in ((0, b_t, 0), (CHUNKS, a_t, 1)):
        product = dot(left[...], grad[...], 1, dim)
        rows = slice(offset, offset + CHUNKS)
        for c in range(NCOL):
            for t in range(TILES):
                spot = slice(t * LANES, (t + 1) * LANES)
                even, odd = swap_halves(
                    product[32 * c : 32 * c + 16, spot], product[32 * c + 16 : 32 * c + 32, spot]
                )
                send[32 * t + c, rows] = even.astype(BF16)
                send[32 * t + 16 + c, rows] = odd.astype(BF16)


def back_kernel(recv, zn_t, factor, terms_in, terms, grad_p):
    for s in range(STEPS):
        here = lanes_of(s)
        for part in range(4):
            rows = slice(part * CH, (part + 1) * CH)
            grad_p[rows, here] = recv[:, lanes_of(s, (part // 2) * PAIRS)] * factor[rows, here]
    terms[: 4 * CH] = dot(grad_p[...], zn_t[...].T, 1, 0).astype(BF16)
    terms[4 * CH :] = terms_in[...]


def last_kernel(grad_p, logit_t, pair, gain, w_proj, w_gate, grad_pair, xs):
    gain_c = column(gain[...])
    xs[...] = pair[...].astype(F32).reshape(PAIRS, CH)

    def step(s):
        here = lanes_of(s)
        grad_zn = dot(w_proj[...], grad_p[:, here], 1, 0) + dot(w_gate[...], logit_t[:, here], 1, 0)
        x = load_chunk(xs, s)
        centred = x - jnp.mean(x, axis=0, keepdims=True)
        inverse = lax.rsqrt(jnp.mean(centred * centred, axis=0, keepdims=True) + EPS)
        normed = centred * inverse
        q = grad_zn * gain_c
        first = jnp.mean(q, axis=0, keepdims=True)
        second = jnp.mean(q * normed, axis=0, keepdims=True)
        store_chunk(xs, s, (q - first - normed * second) * inverse)

    loop(step)
    grad_pair[...] = xs[...].reshape(ROWS, COLS, CH).astype(BF16)


def sum_kernel(parts, out):
    total = parts[...].astype(F32).reshape(DEV // 4, 4 * SHARE, LANES)
    while total.shape[0] > 1:
        half = total.shape[0] // 2
        total = total[:half] + total[half:]
    total = total[0]
    mine = total[:SHARE]
    for n in range(1, 4):
        mine = mine + total[n * SHARE : (n + 1) * SHARE]
    mine = jnp.concatenate([mine * (1.0 / N)] * 8, axis=0).astype(BF16)
    for n in range(DEV // 8):
        out[8 * SHARE * n : 8 * SHARE * (n + 1)] = mine


def split_kernel(sums, grad_proj, grad_gate, grad_out, wide, gate, out, sems):
    copies = []
    for part in range(4):
        spot = slice(part * CH, (part + 1) * CH)
        wide[:, spot] = sums[spot].astype(F32).T
        copies += fetch(sems, part, (wide.at[:, spot], grad_proj.at[:, spot]))
    gate[...] = sums[4 * CH : 5 * CH].astype(F32).T
    copies += fetch(sems, 4, (gate, grad_gate))
    out[...] = sums[5 * CH :].astype(F32)
    copies += fetch(sems, 5, (out, grad_out))
    for copy in copies:
        copy.wait()


def call(kernel, outs, scratch, flops, args, hbm=0, out_space=pltpu.VMEM, vmem=16):
    moved = sum(x.size * x.dtype.itemsize for x in args) + sum(
        x.size * x.dtype.itemsize for x in outs
    )
    spaces = [pltpu.HBM] * hbm + [pltpu.VMEM] * (len(args) - hbm)
    args = [
        pltpu.with_memory_space_constraint(x, pltpu.HBM) if n < hbm else x
        for n, x in enumerate(args)
    ]
    return pl.pallas_call(
        kernel,
        out_shape=outs,
        in_specs=[pl.BlockSpec(memory_space=space) for space in spaces],
        out_specs=[pl.BlockSpec(memory_space=out_space)] * len(outs),
        scratch_shapes=scratch,
        compiler_params=pltpu.CompilerParams(vmem_limit_bytes=vmem << 20),
        cost_estimate=pl.CostEstimate(flops=flops, bytes_accessed=moved, transcendentals=0),
    )(*args)


def exchange(x):
    return lax.all_to_all(x, AXES, 0, 0, tiled=True)


def exchange_terms(x):
    split = x.reshape(DEV, SHARE // 2, 2, LANES)
    return lax.all_to_all(split, AXES[::-1], 0, 0, tiled=True).reshape(x.shape)


def split_rows(x):
    return x.reshape(DEV, -1, LANES)


def join_rows(x):
    return x.reshape(DEV, -1)


def body(
    pair,
    cotangent,
    res_mask,
    chain,
    ln_in_gain,
    ln_in_bias,
    w_proj,
    w_gate,
    chain_bias,
    ln_out_gain,
    ln_out_bias,
    w_out,
):
    S = jax.ShapeDtypeStruct
    V = pltpu.VMEM
    unit = 2 * PAIRS * CH * CH

    def flat(x):
        return x.reshape(1, -1)

    send_ab, zn_t, factor = call(
        front_kernel,
        [S((CH, 2 * PAIRS), BF16), S((CH, PAIRS), BF16), S((4 * CH, PAIRS), BF16)],
        [
            pltpu.SMEM((N,), jnp.int32), V((1, CH), F32), V((1, CH), F32), V((CH, 4 * CH), BF16),
            V((ROWS, COLS, CH), BF16), V((ROWS, COLS, CH), F32), V((4 * CH, CH), BF16),
            pltpu.SemaphoreType.DMA((5,)),
        ],
        4 * unit,
        (res_mask, flat(ln_in_gain), flat(ln_in_bias), w_proj, pair),
        hbm=5,
    )
    recv_ab = exchange(split_rows(send_ab))
    send_mixed, a_t, b_t, grad_update, q, slope = call(
        mix_kernel,
        [
            S((DEV, CHUNKS, LANES), BF16), S((N, N), BF16), S((N, N), BF16),
            S((CH, PAIRS), BF16), S((CH, PAIRS), F32), S((CH, PAIRS), F32),
        ],
        [
            V((TILES, N, LANES), F32), pltpu.SMEM((N,), jnp.int32), V((ROWS, COLS, CH), F32),
            V((CH, CH), BF16), pltpu.SemaphoreType.DMA((1,)),
        ],
        2 * N * N * N + 2 * unit,
        (
            chain, flat(chain_bias), flat(ln_out_gain), w_gate, w_out, cotangent, zn_t, recv_ab,
        ),
        hbm=1,
    )
    send_grad, y = call(
        middle_kernel,
        [S((CH, PAIRS), BF16), S((CH, PAIRS), BF16)],
        [],
        0,
        (join_rows(exchange(send_mixed)), q, flat(ln_out_gain), flat(ln_out_bias)),
    )
    send_back, logit_t, terms_in = call(
        unmix_kernel,
        [S((DEV, 2 * CHUNKS, LANES), BF16), S((CH, PAIRS), BF16), S((2 * CH, CH), BF16)],
        [V((TILES, N, LANES), F32), V((N, N), BF16), V((CH, CH), BF16)],
        4 * N * N * N + 3 * unit,
        (exchange(split_rows(send_grad)), a_t, b_t, zn_t, y, slope, grad_update, w_out),
    )
    terms, grad_p = call(
        back_kernel,
        [S((6 * CH, CH), BF16), S((4 * CH, PAIRS), BF16)],
        [],
        4 * unit,
        (join_rows(exchange(send_back)), zn_t, factor, terms_in),
    )
    parts = exchange_terms(terms)
    (summed,) = call(sum_kernel, [S((6 * CH, CH), BF16)], [], 0, (parts,))
    summed, grad_p, logit_t = lax.optimization_barrier((summed, grad_p, logit_t))
    sums = exchange_terms(summed)
    (grad_pair,) = call(
        last_kernel,
        [S((ROWS, COLS, CH), BF16)],
        [V((PAIRS, CH), F32)],
        5 * unit,
        (grad_p, logit_t, pair, flat(ln_in_gain), w_proj, w_gate),
    )
    grad_proj, grad_gate, grad_out = call(
        split_kernel,
        [S((CH, 4 * CH), F32), S((CH, CH), F32), S((CH, CH), F32)],
        [V((CH, 4 * CH), F32), V((CH, CH), F32), V((CH, CH), F32), pltpu.SemaphoreType.DMA((6,))],
        0,
        (sums,),
        out_space=pltpu.HBM,
    )
    return (grad_pair, grad_proj, grad_gate, grad_out)


def solution(mesh):
    return jax.shard_map(
        body,
        mesh=mesh,
        in_specs=(P("row", "col", None), P("row", "col", None)) + (P(),) * 10,
        out_specs=(P("row", "col", None), P(), P(), P()),
        check_vma=False,
    )
```
